32 devices in a mesh: groups: 2 (over y), lon: 4 (over z), lat: 2 (over x), dp: 2 (over core).
Axes of the slice: x: 2, y: 2, z: 4, core: 2. Of those that a mesh axis runs over, the one named last changes fastest.
Arguments:
- fields: bfloat16 [4, 32, 64, 192], P(('groups', 'dp'), 'lat', 'lon'), parts along dimension 0, may hold values from -6 to 6
- cotangent: bfloat16 [4, 32, 64, 192], P(('groups', 'dp'), 'lat', 'lon'), parts along dimension 0, may hold values from -6 to 6
- ocean_mask: int32 [32, 64], P('lat', 'lon'), may hold values from 0 to 1, as said below
- dw_kernel: float32 [7, 7, 192], replicated, may hold values from -0.875 to 0.875
- dw_bias: float32 [192], replicated, may hold values from -4 to 4
- ln_gain: float32 [192], replicated, may hold values from 0.1 to 1.9
- ln_bias: float32 [192], replicated, may hold values from -3 to 3
- w_in: bfloat16 [192, 768], replicated, may hold values from -0.4375 to 0.4375
- b_in: float32 [768], replicated, may hold values from -3 to 3
- w_out: bfloat16 [768, 192], replicated, may hold values from -0.21875 to 0.21875
- b_out: float32 [192], replicated, may hold values from -3 to 3
- layer_scale: float32 [192], replicated, may hold values from 0.3 to 1.5
Outputs:
- block_out: bfloat16 [4, 32, 64, 192], P(('groups', 'dp'), 'lat', 'lon'), parts along dimension 0
- field_grad: bfloat16 [4, 32, 64, 192], P(('groups', 'dp'), 'lat', 'lon'), parts along dimension 0
- grad_kernel: float32 [14, 7, 192], P('groups'), parts along dimension 0
- grad_dw_bias: float32 [384], P('groups'), parts along dimension 0
- grad_ln_gain: float32 [384], P('groups'), parts along dimension 0
- grad_ln_bias: float32 [384], P('groups'), parts along dimension 0
- grad_w_in: float32 [384, 768], P('groups'), parts along dimension 0
- grad_b_in: float32 [1536], P('groups'), parts along dimension 0
- grad_w_out: float32 [1536, 192], P('groups'), parts along dimension 0
- grad_b_out: float32 [384], P('groups'), parts along dimension 0
- grad_scale: float32 [384], P('groups'), parts along dimension 0
The draws below stay inside these ranges and needn't reach their ends.
There are 2 independent parts, one for each index of `groups`. The reference program is written for one: setup_inputs(seed, part) draws one part's arguments, and reference() takes and returns one part's arrays. A program takes and returns all parts, laid end to end along the dimension named above; an argument that names none is the same for every part. Nothing has to cross between parts.
Inputs may be any that keep to these rules, and one draw needn't show every extreme that they name: `ocean_mask`: each device's tile of 16 x 16 cells holds at most 192 ocean cells, and some tile holds exactly 192.
All inputs are finite; a program needn't handle non-finite values.
Results may differ from the reference program's by a relative error of at most 0.0065.
Values may be sent and summed in bfloat16 or wider, within the bound.
No kernel may reach another device: no remote copies, remote signals or barrier semaphores. Data moves between devices by JAX's collectives and lax.ppermute only.
A program may use at most 64 MiB of HBM per device.

```python
import math
import jax
import jax.numpy as jnp
from jax import lax

C = 192
HID = 768
TH = 16
TW = 16
NH = 32
NW = 64
B = 2
OCEAN_CAP = 192
N_LON = 4
N_LAT = 2


def draw_ocean_mask(key, part):
    cells = TH * TW
    tiles = N_LAT * N_LON
    count_key, order_key = jax.random.split(key)
    counts = jax.random.randint(count_key, (tiles,), OCEAN_CAP // 4, OCEAN_CAP + 1)
    counts = counts.at[0].set(OCEAN_CAP)

    def tile_ranks(tile_key):
        return jax.random.permutation(tile_key, cells)
    ranks = jax.vmap(tile_ranks)(jax.random.split(order_key, tiles))
    mask = (ranks < counts[:, None]).astype(jnp.int32)
    return mask.reshape(N_LAT, N_LON, TH, TW).transpose(0, 2, 1, 3).reshape(TH * N_LAT, TW * N_LON)


def steps_of(own_key, shape, cuts, low, largest):
    factor_of, own = 1.0, jax.random.fold_in(own_key, 6)
    for dim, parts in cuts:
        draws = jnp.exp(jax.random.uniform(jax.random.fold_in(own, dim), (parts,), jnp.float32, low / len(cuts), largest / len(cuts)))
        factor_of = factor_of * jnp.repeat(draws, shape[dim] // parts).reshape([-1 if axis == dim else 1 for axis in range(len(shape))])
    return factor_of


def scatter_about(rng, shape, deviation, limit, cuts=(), held_as=jnp.bfloat16):
    factor_of = steps_of(rng, shape, cuts, -0.22, 0.18) if cuts else 1.0
    drawn = jax.random.normal(rng, shape, jnp.float32) * deviation * factor_of
    return jnp.minimum(jnp.maximum(drawn, -limit), limit).astype(held_as)


def setup_inputs(seed: int = 0, part: int = 0) -> dict:
    splits = jax.random.split(jax.random.key(seed), 13)
    own_keys = jax.random.split(jax.random.fold_in(splits[12], part), 13)
    return {
        "fields": scatter_about(own_keys[0], (B, NH, NW, C), 1.0, 6.0, ((0, 2), (1, 2), (2, 4))),
        "cotangent": scatter_about(own_keys[1], (B, NH, NW, C), 1.0, 6.0, ((0, 2), (1, 2), (2, 4))),
        "ocean_mask": draw_ocean_mask(jax.random.fold_in(splits[12], 71), part),
        "dw_kernel": scatter_about(splits[3], (7, 7, C), 49 ** -0.5, 0.875, (), jnp.float32),
        "dw_bias": scatter_about(splits[4], (C,), 1.0, 4.0, (), jnp.float32),
        "ln_gain": jnp.clip(1.0 + 0.18 * jax.random.normal(splits[5], (C,), jnp.float32), 0.1, 1.9),
        "ln_bias": scatter_about(splits[6], (C,), 0.5, 3.0, (), jnp.float32),
        "w_in": scatter_about(splits[7], (C, HID), C ** -0.5, 0.4375),
        "b_in": scatter_about(splits[8], (HID,), 0.5, 3.0, (), jnp.float32),
        "w_out": scatter_about(splits[9], (HID, C), HID ** -0.5, 0.21875),
        "b_out": scatter_about(splits[10], (C,), 0.5, 3.0, (), jnp.float32),
        "layer_scale": jnp.clip(jnp.exp(jax.random.uniform(splits[11], (C,), jnp.float32, math.log(0.3), math.log(1.5))), 0.3, 1.5),
    }


EPS = 1e-06

def pad_field(field):
    padded = jnp.pad(field, ((3, 3), (0, 0), (0, 0)))
    return jnp.concatenate([padded[:, -3:], padded, padded[:, :3]], axis=1)

def depthwise(padded, kernel, tile_h, tile_w):
    total = jnp.zeros(padded.shape[:-3] + (tile_h, tile_w, padded.shape[-1]), jnp.float32)
    for row_off in range(7):
        for col_off in range(7):
            total = total + padded[..., row_off:row_off + tile_h, col_off:col_off + tile_w, :] * kernel[row_off, col_off]
    return total

def depthwise_back(padded, kernel, tile_h, tile_w):
    total = jnp.zeros(padded.shape[:-3] + (tile_h, tile_w, padded.shape[-1]), jnp.float32)
    for row_off in range(7):
        for col_off in range(7):
            total = total + padded[..., 6 - row_off:6 - row_off + tile_h, 6 - col_off:6 - col_off + tile_w, :] * kernel[row_off, col_off]
    return total

def kernel_grad(grad, padded, tile_h, tile_w):
    lead = tuple(range(grad.ndim - 1))
    return jnp.stack([jnp.stack([lax.optimization_barrier(jnp.sum(grad * padded[..., row_off:row_off + tile_h, col_off:col_off + tile_w, :], axis=lead)) for col_off in range(7)]) for row_off in range(7)])

def gelu_tanh(values):
    return jax.nn.gelu(values, approximate=True)

def norm_forward(conv_out, ln_gain, ln_bias):
    center = lax.optimization_barrier(jnp.mean(conv_out, axis=-1, keepdims=True))
    shifted = conv_out - center
    inv_std = lax.rsqrt(lax.optimization_barrier(jnp.mean(shifted * shifted, axis=-1, keepdims=True)) + EPS)
    normed = shifted * inv_std
    return (normed, inv_std, (normed * ln_gain + ln_bias).astype(jnp.bfloat16))

def norm_backward(act_grad, normed, inv_std, ln_gain):
    scaled = act_grad * ln_gain
    return inv_std * (scaled - lax.optimization_barrier(jnp.mean(scaled, axis=-1, keepdims=True)) - normed * lax.optimization_barrier(jnp.mean(scaled * normed, axis=-1, keepdims=True)))

def mlp_pass(act_rows, out_grad, w_in, b_in, w_out, b_out, layer_scale):
    pre = jnp.dot(act_rows, w_in, preferred_element_type=jnp.float32) + b_in
    hidden, gelu_back = jax.vjp(gelu_tanh, pre)
    hidden_b = hidden.astype(jnp.bfloat16)
    branch = jnp.dot(hidden_b, w_out, preferred_element_type=jnp.float32) + b_out
    branch_grad = out_grad * layer_scale
    branch_b = branch_grad.astype(jnp.bfloat16)
    hidden_grad = jnp.dot(branch_b, w_out.T, preferred_element_type=jnp.float32)
    pre_grad = gelu_back(hidden_grad)[0]
    pre_b = pre_grad.astype(jnp.bfloat16)
    act_grad = jnp.dot(pre_b, w_in.T, preferred_element_type=jnp.float32)
    grads = (jnp.dot(act_rows.T, pre_b, preferred_element_type=jnp.float32), lax.optimization_barrier(jnp.sum(pre_grad, axis=0)), jnp.dot(hidden_b.T, branch_b, preferred_element_type=jnp.float32), lax.optimization_barrier(jnp.sum(branch_grad, axis=0)), lax.optimization_barrier(jnp.sum(out_grad * branch, axis=0)))
    return (branch, act_grad, grads)

def reference(fields, cotangent, ocean_mask, dw_kernel, dw_bias, ln_gain, ln_bias, w_in, b_in, w_out, b_out, layer_scale):
    ocean = ocean_mask.astype(jnp.float32)[:, :, None]
    row_count = NH * NW
    block = math.gcd(row_count, 8192)

    def snapshot(carry, inputs):
        field, cot = inputs
        start = field.astype(jnp.float32) * ocean
        padded = pad_field(start)
        conv_out = depthwise(padded, dw_kernel, NH, NW) + dw_bias
        normed, inv_std, act = norm_forward(conv_out, ln_gain, ln_bias)
        out_grad = cot.astype(jnp.float32) * ocean

        def step(acc, pair):
            branch, act_grad, grads = mlp_pass(pair[0], pair[1], w_in, b_in, w_out, b_out, layer_scale)
            return (tuple((old + new for old, new in zip(acc, grads))), (branch, act_grad))
        zeros_mlp = (jnp.zeros((C, HID), jnp.float32), jnp.zeros((HID,), jnp.float32), jnp.zeros((HID, C), jnp.float32), jnp.zeros((C,), jnp.float32), jnp.zeros((C,), jnp.float32))
        mlp_sums, (branch, act_grad) = lax.scan(step, zeros_mlp, (act.reshape(row_count // block, block, C), out_grad.reshape(row_count // block, block, C)))
        branch = branch.reshape(NH, NW, C)
        act_grad = act_grad.reshape(NH, NW, C)
        block_out = (ocean * (start + layer_scale * branch)).astype(jnp.bfloat16)
        conv_grad = norm_backward(act_grad, normed, inv_std, ln_gain)
        local = (kernel_grad(conv_grad, padded, NH, NW), lax.optimization_barrier(jnp.sum(conv_grad, axis=(0, 1))), lax.optimization_barrier(jnp.sum(act_grad * normed, axis=(0, 1))), lax.optimization_barrier(jnp.sum(act_grad, axis=(0, 1)))) + mlp_sums
        field_grad = (ocean * (out_grad + depthwise_back(pad_field(conv_grad), dw_kernel, NH, NW))).astype(jnp.bfloat16)
        return (tuple((old + new for old, new in zip(carry, local))), (block_out, field_grad))
    init = (jnp.zeros((7, 7, C), jnp.float32), jnp.zeros((C,), jnp.float32), jnp.zeros((C,), jnp.float32), jnp.zeros((C,), jnp.float32), jnp.zeros((C, HID), jnp.float32), jnp.zeros((HID,), jnp.float32), jnp.zeros((HID, C), jnp.float32), jnp.zeros((C,), jnp.float32), jnp.zeros((C,), jnp.float32))
    sums, (block_out, field_grad) = lax.scan(snapshot, init, (fields, cotangent))
    factor = 1.0 / math.sqrt(B * NH * NW)
    return (block_out, field_grad, sums[0] * factor, sums[1] * factor, sums[2] * factor, sums[3] * factor, sums[4] * factor, sums[5] * factor, sums[6] * factor, sums[7] * factor, sums[8] * factor)
```

```python
import math

import jax
import jax.numpy as jnp
from jax import lax
from jax.sharding import PartitionSpec as P

EPS = 1e-06


def padded_2(block, sides, width, periodic):
    for axis, dim in sides:
        count = lax.axis_size(axis)
        if count == 2 and not periodic:
            block = padded_pair(block, axis, dim, width)
            continue
        forward = [(i, i + 1) for i in range(count - 1)]
        if periodic:
            forward.append((count - 1, 0))
        backward = [(target, source) for source, target in forward]
        low = lax.ppermute(
            lax.slice_in_dim(block, block.shape[dim] - width, None, axis=dim), axis, forward
        )
        high = lax.ppermute(lax.slice_in_dim(block, 0, width, axis=dim), axis, backward)
        block = jnp.concatenate([low, block, high], axis=dim)
    return block


def padded_pair(block, axis, dim, width):
    first = lax.axis_index(axis) == 0
    head = lax.slice_in_dim(block, 0, width, axis=dim)
    tail = lax.slice_in_dim(block, block.shape[dim] - width, None, axis=dim)
    other = lax.ppermute(jnp.where(first, tail, head), axis, [(0, 1), (1, 0)])
    none = jnp.zeros_like(other)
    return jnp.concatenate(
        [jnp.where(first, none, other), block, jnp.where(first, other, none)], axis=dim
    )


LANES = 256
LINK = jnp.bfloat16


def to_rows(piece):
    rows, columns = piece.shape
    blocks = -(-columns // LANES)
    piece = jnp.pad(piece, ((0, 0), (0, blocks * LANES - columns)))
    return [piece[:, b * LANES : (b + 1) * LANES] for b in range(blocks)]


def from_rows(rows_array, start, rows, columns):
    blocks = -(-columns // LANES)
    parts = [rows_array[start + b * rows : start + (b + 1) * rows] for b in range(blocks)]
    return jnp.concatenate(parts, axis=1)[:, :columns], start + blocks * rows


def rounds_of(count):
    if count & (count - 1) == 0 and count <= 4:
        return [([(i, i ^ step) for i in range(count)], lambda me, s=step: (me ^ s, me ^ s)) for step in range(1, count)]
    return [
        (
            [(i, (i + step) % count) for i in range(count)],
            lambda me, s=step: (lax.rem(me + s, count), lax.rem(me + count - s, count)),
        )
        for step in range(1, count)
    ]


def scatter_sum(rows_array, axis):
    count = lax.axis_size(axis)
    size = rows_array.shape[0] // count
    me = lax.axis_index(axis)
    total = lax.dynamic_slice_in_dim(rows_array, me * size, size, axis=0)
    arrived = []
    for perm, ends in rounds_of(count):
        target, _ = ends(me)
        piece = lax.dynamic_slice_in_dim(rows_array, target * size, size, axis=0)
        arrived.append(lax.ppermute(piece.astype(LINK), axis, perm))
    for piece in arrived:
        total = total + piece.astype(jnp.float32)
    return total


def gather_rows(piece, axis):
    count = lax.axis_size(axis)
    size = piece.shape[0]
    me = lax.axis_index(axis)
    whole = jnp.zeros((count * size,) + piece.shape[1:], piece.dtype)
    whole = lax.dynamic_update_slice_in_dim(whole, piece, me * size, axis=0)
    for perm, ends in rounds_of(count):
        _, source = ends(me)
        other = lax.ppermute(piece, axis, perm)
        whole = lax.dynamic_update_slice_in_dim(whole, other, source * size, axis=0)
    return whole


def sum_over(pieces, axes, factor):
    members = math.prod(lax.axis_size(axis) for axis in axes)
    stacked = sum((to_rows(piece) for piece in pieces), [])
    rows = sum(part.shape[0] for part in stacked)
    quantum = members * 8
    extra = -rows % quantum
    stacked.append(jnp.zeros((extra, LANES), jnp.float32))
    total = jnp.concatenate(stacked, axis=0)
    for axis in axes:
        total = scatter_sum(total, axis)
    total = (total * factor).astype(LINK)
    for axis in reversed(axes):
        total = gather_rows(total, axis)
    total = total.astype(jnp.float32)
    out, start = [], 0
    for piece in pieces:
        value, start = from_rows(total, start, *piece.shape)
        out.append(value)
    return out


def depthwise(padded, kernel, tile_h, tile_w):
    total = jnp.zeros(padded.shape[:-3] + (tile_h, tile_w, padded.shape[-1]), jnp.float32)
    for row_off in range(7):
        for col_off in range(7):
            total = (
                total
                + padded[..., row_off : row_off + tile_h, col_off : col_off + tile_w, :]
                * kernel[row_off, col_off]
            )
    return total


def depthwise_back(padded, kernel, tile_h, tile_w):
    total = jnp.zeros(padded.shape[:-3] + (tile_h, tile_w, padded.shape[-1]), jnp.float32)
    for row_off in range(7):
        for col_off in range(7):
            total = (
                total
                + padded[
                    ..., 6 - row_off : 6 - row_off + tile_h, 6 - col_off : 6 - col_off + tile_w, :
                ]
                * kernel[row_off, col_off]
            )
    return total


def kernel_grad(grad, padded, tile_h, tile_w):
    lead = tuple(range(grad.ndim - 1))
    return jnp.stack(
        [
            jnp.stack(
                [
                    jnp.sum(
                        grad
                        * padded[..., row_off : row_off + tile_h, col_off : col_off + tile_w, :],
                        axis=lead,
                    )
                    for col_off in range(7)
                ]
            )
            for row_off in range(7)
        ]
    )


def gelu_tanh(values):
    return jax.nn.gelu(values, approximate=True)


def mlp_pass(act_rows, out_grad, w_in, b_in, w_out, b_out, layer_scale):
    pre = jnp.dot(act_rows, w_in, preferred_element_type=jnp.float32) + b_in
    hidden, gelu_back = jax.vjp(gelu_tanh, pre)
    hidden_b = hidden.astype(jnp.bfloat16)
    branch = jnp.dot(hidden_b, w_out, preferred_element_type=jnp.float32) + b_out
    branch_grad = out_grad * layer_scale
    branch_b = branch_grad.astype(jnp.bfloat16)
    hidden_grad = jnp.dot(branch_b, w_out.T, preferred_element_type=jnp.float32)
    pre_grad = gelu_back(hidden_grad)[0]
    pre_b = pre_grad.astype(jnp.bfloat16)
    act_grad = jnp.dot(pre_b, w_in.T, preferred_element_type=jnp.float32)
    grads = (
        jnp.dot(act_rows.T, pre_b, preferred_element_type=jnp.float32),
        jnp.sum(pre_grad, axis=0),
        jnp.dot(branch_b.T, hidden_b, preferred_element_type=jnp.float32),
        jnp.sum(branch_grad, axis=0),
        jnp.sum(out_grad * branch, axis=0),
    )
    return (branch, act_grad, grads)


def body(
    fields,
    cotangent,
    ocean_mask,
    dw_kernel,
    dw_bias,
    ln_gain,
    ln_bias,
    w_in,
    b_in,
    w_out,
    b_out,
    layer_scale,
):
    snapshots, tile_h, tile_w, channels = fields.shape
    cells = tile_h * tile_w
    ocean = ocean_mask.astype(jnp.float32)[None, :, :, None]
    start_b = fields * ocean_mask.astype(jnp.bfloat16)[None, :, :, None]
    lat_ext = padded_2(start_b, (("lat", 1),), 3, False)
    padded = padded_2(lat_ext, (("lon", 2),), 3, True).astype(jnp.float32)
    start = start_b.astype(jnp.float32)
    conv_out = depthwise(padded, dw_kernel, tile_h, tile_w) + dw_bias
    center = jnp.mean(conv_out, axis=-1, keepdims=True)
    shifted = conv_out - center
    inv_std = lax.rsqrt(jnp.mean(shifted * shifted, axis=-1, keepdims=True) + EPS)
    normed = shifted * inv_std
    act = (normed * ln_gain + ln_bias).astype(jnp.bfloat16)
    out_grad = cotangent.astype(jnp.float32) * ocean
    flat_branch, flat_act_grad, mlp_sums = mlp_pass(
        act.reshape(-1, channels),
        out_grad.reshape(-1, channels),
        w_in,
        b_in,
        w_out,
        b_out,
        layer_scale,
    )
    branch = flat_branch.reshape(fields.shape)
    act_grad = flat_act_grad.reshape(fields.shape)
    block_out = (ocean * (start + layer_scale * branch)).astype(jnp.bfloat16)
    scaled = act_grad * ln_gain
    conv_grad = inv_std * (
        scaled
        - jnp.mean(scaled, axis=-1, keepdims=True)
        - normed * jnp.mean(scaled * normed, axis=-1, keepdims=True)
    )
    grad_lat = padded_2(conv_grad.astype(jnp.bfloat16), (("lat", 1),), 3, False).astype(
        conv_grad.dtype
    )
    grad_padded = padded_2(grad_lat.astype(jnp.bfloat16), (("lon", 2),), 3, True).astype(
        grad_lat.dtype
    )
    field_grad = (
        ocean * (out_grad + depthwise_back(grad_padded, dw_kernel, tile_h, tile_w))
    ).astype(jnp.bfloat16)
    lead = (0, 1, 2)
    local = (
        kernel_grad(conv_grad, padded, tile_h, tile_w),
        jnp.sum(conv_grad, axis=lead),
        jnp.sum(act_grad * normed, axis=lead),
        jnp.sum(act_grad, axis=lead),
    ) + mlp_sums
    members = lax.axis_size("lon") * lax.axis_size("lat") * lax.axis_size("dp")
    factor = 1.0 / math.sqrt(snapshots * cells * members)
    hid = w_in.shape[1]
    smalls = jnp.concatenate(
        [
            local[0].reshape(-1, channels),
            jnp.stack([local[1], local[2], local[3], local[7], local[8]]),
            local[5].reshape(-1, channels),
        ],
        axis=0,
    )
    got = sum_over([local[4], local[6], smalls], ("dp", "lat", "lon"), factor)
    taps = dw_kernel.shape[0] * dw_kernel.shape[1]
    small = got[2]
    finals = (
        small[:taps].reshape(dw_kernel.shape),
        small[taps],
        small[taps + 1],
        small[taps + 2],
        got[0],
        small[taps + 5 :].reshape(hid),
        got[1].T,
        small[taps + 3],
        small[taps + 4],
    )
    return (
        block_out,
        field_grad,
        finals[0],
        finals[1],
        finals[2],
        finals[3],
        finals[4],
        finals[5],
        finals[6],
        finals[7],
        finals[8],
    )


def solution(mesh):
    return jax.shard_map(
        body,
        mesh=mesh,
        in_specs=(
            P(("groups", "dp"), "lat", "lon", None),
            P(("groups", "dp"), "lat", "lon", None),
            P("lat", "lon"),
            P(),
            P(),
            P(),
            P(),
            P(),
            P(),
            P(),
            P(),
            P(),
        ),
        out_specs=(
            P(("groups", "dp"), "lat", "lon", None),
            P(("groups", "dp"), "lat", "lon", None),
            P("groups", None, None),
            P("groups"),
            P("groups"),
            P("groups"),
            P("groups", None),
            P("groups"),
            P("groups", None),
            P("groups"),
            P("groups"),
        ),
        check_vma=False,
    )
```

```python
import functools
import math

import jax
import jax.numpy as jnp
from jax import lax
from jax.experimental import pallas as pl
from jax.experimental.pallas import tpu as pltpu
from jax.sharding import PartitionSpec as P

EPS = 1e-06


def padded_2(block, sides, width, periodic):
    for axis, dim in sides:
        count = lax.axis_size(axis)
        if count == 2 and not periodic:
            block = padded_pair(block, axis, dim, width)
            continue
        forward = [(i, i + 1) for i in range(count - 1)]
        if periodic:
            forward.append((count - 1, 0))
        backward = [(target, source) for source, target in forward]
        low = lax.ppermute(
            lax.slice_in_dim(block, block.shape[dim] - width, None, axis=dim), axis, forward
        )
        high = lax.ppermute(lax.slice_in_dim(block, 0, width, axis=dim), axis, backward)
        block = jnp.concatenate([low, block, high], axis=dim)
    return block


def padded_pair(block, axis, dim, width):
    first = lax.axis_index(axis) == 0
    head = lax.slice_in_dim(block, 0, width, axis=dim)
    tail = lax.slice_in_dim(block, block.shape[dim] - width, None, axis=dim)
    other = lax.ppermute(jnp.where(first, tail, head), axis, [(0, 1), (1, 0)])
    none = jnp.zeros_like(other)
    return jnp.concatenate(
        [jnp.where(first, none, other), block, jnp.where(first, other, none)], axis=dim
    )


LANES = 256
LINK = jnp.bfloat16


def to_rows(piece):
    rows, columns = piece.shape
    blocks = -(-columns // LANES)
    piece = jnp.pad(piece, ((0, 0), (0, blocks * LANES - columns)))
    return [piece[:, b * LANES : (b + 1) * LANES] for b in range(blocks)]


def from_rows(rows_array, start, rows, columns):
    blocks = -(-columns // LANES)
    parts = [rows_array[start + b * rows : start + (b + 1) * rows] for b in range(blocks)]
    return jnp.concatenate(parts, axis=1)[:, :columns], start + blocks * rows


def rounds_of(count):
    if count & (count - 1) == 0 and count <= 4:
        return [([(i, i ^ step) for i in range(count)], lambda me, s=step: (me ^ s, me ^ s)) for step in range(1, count)]
    return [
        (
            [(i, (i + step) % count) for i in range(count)],
            lambda me, s=step: (lax.rem(me + s, count), lax.rem(me + count - s, count)),
        )
        for step in range(1, count)
    ]


def scatter_sum(rows_array, axis):
    count = lax.axis_size(axis)
    size = rows_array.shape[0] // count
    me = lax.axis_index(axis)
    total = lax.dynamic_slice_in_dim(rows_array, me * size, size, axis=0)
    arrived = []
    for perm, ends in rounds_of(count):
        target, _ = ends(me)
        piece = lax.dynamic_slice_in_dim(rows_array, target * size, size, axis=0)
        arrived.append(lax.ppermute(piece.astype(LINK), axis, perm))
    for piece in arrived:
        total = total + piece.astype(jnp.float32)
    return total


def gather_rows(piece, axis):
    count = lax.axis_size(axis)
    size = piece.shape[0]
    me = lax.axis_index(axis)
    whole = jnp.zeros((count * size,) + piece.shape[1:], piece.dtype)
    whole = lax.dynamic_update_slice_in_dim(whole, piece, me * size, axis=0)
    for perm, ends in rounds_of(count):
        _, source = ends(me)
        other = lax.ppermute(piece, axis, perm)
        whole = lax.dynamic_update_slice_in_dim(whole, other, source * size, axis=0)
    return whole


def sum_over(pieces, axes, factor):
    members = math.prod(lax.axis_size(axis) for axis in axes)
    stacked = sum((to_rows(piece) for piece in pieces), [])
    rows = sum(part.shape[0] for part in stacked)
    quantum = members * 8
    extra = -rows % quantum
    stacked.append(jnp.zeros((extra, LANES), jnp.float32))
    total = jnp.concatenate(stacked, axis=0)
    for axis in axes:
        total = scatter_sum(total, axis)
    total = (total * factor).astype(LINK)
    for axis in reversed(axes):
        total = gather_rows(total, axis)
    total = total.astype(jnp.float32)
    out, start = [], 0
    for piece in pieces:
        value, start = from_rows(total, start, *piece.shape)
        out.append(value)
    return out


def depthwise(padded, kernel, tile_h, tile_w):
    total = jnp.zeros(padded.shape[:-3] + (tile_h, tile_w, padded.shape[-1]), jnp.float32)
    for row_off in range(7):
        for col_off in range(7):
            total = (
                total
                + padded[..., row_off : row_off + tile_h, col_off : col_off + tile_w, :]
                * kernel[row_off, col_off]
            )
    return total


def depthwise_back(padded, kernel, tile_h, tile_w):
    total = jnp.zeros(padded.shape[:-3] + (tile_h, tile_w, padded.shape[-1]), jnp.float32)
    for row_off in range(7):
        for col_off in range(7):
            total = (
                total
                + padded[
                    ..., 6 - row_off : 6 - row_off + tile_h, 6 - col_off : 6 - col_off + tile_w, :
                ]
                * kernel[row_off, col_off]
            )
    return total


def kernel_grad(grad, padded, tile_h, tile_w):
    lead = tuple(range(grad.ndim - 1))
    return jnp.stack(
        [
            jnp.stack(
                [
                    jnp.sum(
                        grad
                        * padded[..., row_off : row_off + tile_h, col_off : col_off + tile_w, :],
                        axis=lead,
                    )
                    for col_off in range(7)
                ]
            )
            for row_off in range(7)
        ]
    )


def gelu_tanh(values):
    return jax.nn.gelu(values, approximate=True)


def mlp_pass(act_rows, out_grad, w_in, b_in, w_out, b_out, layer_scale):
    pre = jnp.dot(act_rows, w_in, preferred_element_type=jnp.float32) + b_in
    hidden, gelu_back = jax.vjp(gelu_tanh, pre)
    hidden_b = hidden.astype(jnp.bfloat16)
    branch = jnp.dot(hidden_b, w_out, preferred_element_type=jnp.float32) + b_out
    branch_grad = out_grad * layer_scale
    branch_b = branch_grad.astype(jnp.bfloat16)
    hidden_grad = jnp.dot(branch_b, w_out.T, preferred_element_type=jnp.float32)
    pre_grad = gelu_back(hidden_grad)[0]
    pre_b = pre_grad.astype(jnp.bfloat16)
    act_grad = jnp.dot(pre_b, w_in.T, preferred_element_type=jnp.float32)
    grads = (
        jnp.dot(act_rows.T, pre_b, preferred_element_type=jnp.float32),
        jnp.sum(pre_grad, axis=0),
        jnp.dot(branch_b.T, hidden_b, preferred_element_type=jnp.float32),
        jnp.sum(branch_grad, axis=0),
        jnp.sum(out_grad * branch, axis=0),
    )
    return (branch, act_grad, grads)


def body(
    fields,
    cotangent,
    ocean_mask,
    dw_kernel,
    dw_bias,
    ln_gain,
    ln_bias,
    w_in,
    b_in,
    w_out,
    b_out,
    layer_scale,
):
    snapshots, tile_h, tile_w, channels = fields.shape
    cells = tile_h * tile_w
    ocean = ocean_mask.astype(jnp.float32)[None, :, :, None]
    start_b = fields * ocean_mask.astype(jnp.bfloat16)[None, :, :, None]
    lat_ext = padded_2(start_b, (("lat", 1),), 3, False)
    padded = padded_2(lat_ext, (("lon", 2),), 3, True).astype(jnp.float32)
    start = start_b.astype(jnp.float32)
    conv_out = depthwise(padded, dw_kernel, tile_h, tile_w) + dw_bias
    center = jnp.mean(conv_out, axis=-1, keepdims=True)
    shifted = conv_out - center
    inv_std = lax.rsqrt(jnp.mean(shifted * shifted, axis=-1, keepdims=True) + EPS)
    normed = shifted * inv_std
    act = (normed * ln_gain + ln_bias).astype(jnp.bfloat16)
    out_grad = cotangent.astype(jnp.float32) * ocean
    flat_branch, flat_act_grad, mlp_sums = mlp_pass(
        act.reshape(-1, channels),
        out_grad.reshape(-1, channels),
        w_in,
        b_in,
        w_out,
        b_out,
        layer_scale,
    )
    branch = flat_branch.reshape(fields.shape)
    act_grad = flat_act_grad.reshape(fields.shape)
    block_out = (ocean * (start + layer_scale * branch)).astype(jnp.bfloat16)
    scaled = act_grad * ln_gain
    conv_grad = inv_std * (
        scaled
        - jnp.mean(scaled, axis=-1, keepdims=True)
        - normed * jnp.mean(scaled * normed, axis=-1, keepdims=True)
    )
    grad_lat = padded_2(conv_grad.astype(jnp.bfloat16), (("lat", 1),), 3, False).astype(
        conv_grad.dtype
    )
    grad_padded = padded_2(grad_lat.astype(jnp.bfloat16), (("lon", 2),), 3, True).astype(
        grad_lat.dtype
    )
    field_grad = (
        ocean * (out_grad + depthwise_back(grad_padded, dw_kernel, tile_h, tile_w))
    ).astype(jnp.bfloat16)
    lead = (0, 1, 2)
    local = (
        kernel_grad(conv_grad, padded, tile_h, tile_w),
        jnp.sum(conv_grad, axis=lead),
        jnp.sum(act_grad * normed, axis=lead),
        jnp.sum(act_grad, axis=lead),
    ) + mlp_sums
    members = lax.axis_size("lon") * lax.axis_size("lat") * lax.axis_size("dp")
    factor = 1.0 / math.sqrt(snapshots * cells * members)
    hid = w_in.shape[1]
    smalls = jnp.concatenate(
        [
            local[0].reshape(-1, channels),
            jnp.stack([local[1], local[2], local[3], local[7], local[8]]),
            local[5].reshape(-1, channels),
        ],
        axis=0,
    )
    got = sum_over([local[4], local[6], smalls], ("dp", "lat", "lon"), factor)
    taps = dw_kernel.shape[0] * dw_kernel.shape[1]
    small = got[2]
    finals = (
        small[:taps].reshape(dw_kernel.shape),
        small[taps],
        small[taps + 1],
        small[taps + 2],
        got[0],
        small[taps + 5 :].reshape(hid),
        got[1].T,
        small[taps + 3],
        small[taps + 4],
    )
    return (
        block_out,
        field_grad,
        finals[0],
        finals[1],
        finals[2],
        finals[3],
        finals[4],
        finals[5],
        finals[6],
        finals[7],
        finals[8],
    )


VMEM = pl.BlockSpec(memory_space=pltpu.VMEM)
HBM = pl.BlockSpec(memory_space=pltpu.HBM)
PARAMS = pltpu.CompilerParams(vmem_limit_bytes=20 << 20)
F32 = jnp.float32
SLOT = 256
STRIDE = 32
CENTER = 8
PAD_ROWS = 24
ROOT_2_PI = math.sqrt(2 / math.pi)


def call(kernel, outs, args, flops=0, scratch=(), hbm=(), hbm_out=()):
    moved = sum(a.size * a.dtype.itemsize for a in args) + sum(
        math.prod(s) * jnp.dtype(d).itemsize for s, d in outs
    )
    return pl.pallas_call(
        kernel,
        out_shape=tuple(jax.ShapeDtypeStruct(s, d) for s, d in outs),
        in_specs=[HBM if i in hbm else VMEM for i in range(len(args))],
        out_specs=tuple(HBM if i in hbm_out else VMEM for i in range(len(outs))),
        scratch_shapes=list(scratch),
        compiler_params=PARAMS,
        cost_estimate=pl.CostEstimate(flops=flops, bytes_accessed=moved, transcendentals=0),
    )(*args)


def copies(pairs, sems):
    started = [
        pltpu.make_async_copy(source, target, sems.at[i]) for i, (source, target) in enumerate(pairs)
    ]
    for copy in started:
        copy.start()
    return started


def dot(a, b, dims):
    return lax.dot_general(a, b, (dims, ((), ())), preferred_element_type=F32)


def tap_slots(taps):
    return [((i // 24) * 8 + i % 8, ((i % 24) // 8) * SLOT) for i in range(taps)]


def mask_full(mask_ref, cells, channels):
    tile_w = mask_ref.shape[1]
    index = lax.broadcasted_iota(jnp.int32, (cells, mask_ref.shape[0]), 0)
    of_row = lax.div(index, tile_w) == lax.broadcasted_iota(jnp.int32, index.shape, 1)
    mask = mask_ref[...].astype(F32).astype(LINK)
    rows = dot(of_row.astype(F32).astype(LINK), mask, ((1,), (0,)))
    index = lax.broadcasted_iota(jnp.int32, rows.shape, 0)
    of_col = lax.rem(index, tile_w) == lax.broadcasted_iota(jnp.int32, rows.shape, 1)
    picked = jnp.where(of_col, rows, 0.0).astype(LINK)
    return dot(picked, jnp.ones((tile_w, channels), LINK), ((1,), (0,)))


def prepare_kernel(tw, fields_hbm, mask_hbm, start_ref, edge_ref, full_ref, fields_ref, mask_ref, sems):
    fetch = copies(((mask_hbm, mask_ref), (fields_hbm, fields_ref)), sems)
    cells, channels = fields_ref.shape
    fetch[0].wait()
    full = mask_full(mask_ref, cells, channels)
    full_ref[...] = full
    fetch[1].wait()
    start_ref[...] = (fields_ref[...].astype(F32) * full).astype(LINK)
    first = lax.axis_index("lat") == 0
    edge_ref[...] = jnp.where(first, start_ref[cells - 3 * tw :], start_ref[: 3 * tw])


def load_kernel(full_ref, *refs):
    count = (len(refs) - 3) // 2
    sources, targets = refs[:count], refs[count : 2 * count]
    branch_grad_ref, hidden_grad_ref, sems = refs[2 * count :]
    fetch = copies(tuple(zip(sources, targets)), sems)
    cot_ref, scale_ref, w_out_ref = targets[:3]
    for copy in fetch[:3]:
        copy.wait()
    grad = (cot_ref[...].astype(F32) * full_ref[...] * scale_ref[...]).astype(LINK)
    branch_grad_ref[...] = grad
    hidden_grad_ref[...] = dot(grad, w_out_ref[...], ((1,), (0,)))
    for copy in fetch[3:]:
        copy.wait()


def lane_tiles(channels):
    return [(t, t * 128, min(128, channels - t * 128)) for t in range(-(-channels // 128))]


def put_rows(padded_ref, row, values):
    for t, lane, width in lane_tiles(values.shape[1]):
        padded_ref[t, pl.ds(row, values.shape[0]), pl.ds(0, width)] = values[:, lane : lane + width]


def fill_center(padded_ref, value_of_row, tile_h, tw, top, bottom):
    for h in range(tile_h):
        put_rows(padded_ref, (h + 3) * STRIDE + CENTER, value_of_row(h))
    for r in range(3):
        put_rows(padded_ref, r * STRIDE + CENTER, top(r))
        put_rows(padded_ref, (tile_h + 3 + r) * STRIDE + CENTER, bottom(r))


def write_edges(padded_ref, tw, channels, near_ref, far_ref, row):
    even = lax.rem(lax.axis_index("lon"), 2) == 0
    for c in range(3):
        for t, lane, width in lane_tiles(channels):
            left = padded_ref[t, pl.ds(CENTER + c, PAD_ROWS, stride=STRIDE), :]
            right = padded_ref[t, pl.ds(CENTER + tw - 3 + c, PAD_ROWS, stride=STRIDE), :]
            place = pl.ds(row, PAD_ROWS), pl.ds(c * SLOT + lane, width)
            near_ref[place] = jnp.where(even, right, left)[:, :width].astype(LINK)
            far_ref[place] = jnp.where(even, left, right)[:, :width].astype(LINK)


def read_edges(padded_ref, tw, channels, near_ref, far_ref, row):
    even = lax.rem(lax.axis_index("lon"), 2) == 0
    for c in range(3):
        for t, lane, width in lane_tiles(channels):
            place = pl.ds(row, PAD_ROWS), pl.ds(c * SLOT + lane, 128)
            near = near_ref[place].astype(F32)
            far = far_ref[place].astype(F32)
            left = pl.ds(CENTER - 3 + c, PAD_ROWS, stride=STRIDE)
            right = pl.ds(CENTER + tw + c, PAD_ROWS, stride=STRIDE)
            padded_ref[t, left, :] = jnp.where(even, far, near)
            padded_ref[t, right, :] = jnp.where(even, near, far)


def lat_rows(read, tw):
    first = lax.axis_index("lat") == 0

    def top(r):
        rows = read(r).astype(F32)
        return jnp.where(first, jnp.zeros_like(rows), rows)

    def bottom(r):
        rows = read(r).astype(F32)
        return jnp.where(first, rows, jnp.zeros_like(rows))

    return top, bottom


def shift_all(padded_ref, shifts_ref, tile_h, tw):
    for q in range(7):
        for h in range(tile_h + 6):
            for t, lane, width in lane_tiles(shifts_ref.shape[2]):
                shifts_ref[q, pl.ds(h * tw, tw), pl.ds(lane, width)] = padded_ref[
                    t, pl.ds(h * STRIDE + CENTER - 3 + q, tw), pl.ds(0, width)
                ]


def convolve(shifts_ref, kernel_ref, out_ref, tile_h, tw, flip):
    block = 2

    def step(i, carry):
        base = pl.multiple_of(i * block * tw, 8)
        total = jnp.zeros((block * tw, out_ref.shape[1]), F32)
        for q in range(7):
            rows = shifts_ref[q, pl.ds(base, (block + 6) * tw), :]
            for r in range(7):
                tap = kernel_ref[6 - r, 6 - q : 7 - q, :] if flip else kernel_ref[r, q : q + 1, :]
                total = total + rows[r * tw : (r + block) * tw] * tap
        out_ref[pl.ds(base, block * tw), :] = total
        return carry

    lax.fori_loop(0, tile_h // block, step, 0)


def edges_kernel(tile_h, tw, start_ref, lat_ref, loaded_ref, near_ref, far_ref, padded_ref):
    top, bottom = lat_rows(lambda r: lat_ref[pl.ds(r * tw, tw), :], tw)
    fill_center(
        padded_ref, lambda h: start_ref[pl.ds(h * tw, tw), :].astype(F32), tile_h, tw, top, bottom
    )
    write_edges(padded_ref, tw, start_ref.shape[1], near_ref, far_ref, 0)


def inner_conv_kernel(
    tile_h, tw, start_ref, lat_ref, kernel_ref, bias_ref, out_ref, padded_ref, shifts_ref, conv_ref
):
    top, bottom = lat_rows(lambda r: lat_ref[pl.ds(r * tw, tw), :], tw)
    fill_center(
        padded_ref, lambda h: start_ref[pl.ds(h * tw, tw), :].astype(F32), tile_h, tw, top, bottom
    )
    blank = jnp.zeros((PAD_ROWS, 128), F32)
    for t in range(padded_ref.shape[0]):
        for c in range(3):
            padded_ref[t, pl.ds(CENTER - 3 + c, PAD_ROWS, stride=STRIDE), :] = blank
            padded_ref[t, pl.ds(CENTER + tw + c, PAD_ROWS, stride=STRIDE), :] = blank
    shift_all(padded_ref, shifts_ref, tile_h, tw)
    convolve(shifts_ref, kernel_ref, conv_ref, tile_h, tw, False)
    conv = conv_ref[...] + bias_ref[...]
    for t, lane, width in lane_tiles(conv.shape[1]):
        out_ref[t, :, pl.ds(0, width)] = conv[:, lane : lane + width]


def add_columns(conv_ref, kernel_ref, near_ref, far_ref, tile_h, tw, channels):
    even = lax.rem(lax.axis_index("lon"), 2) == 0
    for t, lane, width in lane_tiles(channels):
        left, right = [], []
        for c in range(3):
            place = pl.ds(0, PAD_ROWS), pl.ds(c * SLOT + lane, width)
            near = near_ref[place].astype(F32)
            far = far_ref[place].astype(F32)
            left.append(jnp.where(even, far, near))
            right.append(jnp.where(even, near, far))
        for w in range(3):
            for col, halo, taps in (
                (w, left, [(q, w + q) for q in range(3 - w)]),
                (tw - 1 - w, right, [(6 - q, 2 - w - q) for q in range(3 - w)]),
            ):
                rows = pl.ds(col, tile_h, stride=tw)
                total = conv_ref[t, rows, :][:, :width]
                for q, c in taps:
                    for r in range(7):
                        tap = kernel_ref[r, q : q + 1, pl.ds(lane, width)]
                        total = total + halo[c][r : r + tile_h] * tap
                conv_ref[t, rows, pl.ds(0, width)] = total


def main_kernel(
    tile_h, tw,
    inner_ref, near_ref, far_ref, kernel_ref, gain_ref, ln_bias_ref, branch_grad_ref, hidden_grad_ref,
    w_in_ref, b_in_ref,
    send_ref, keep_ref, normed_ref, inv_std_ref, hidden_ref, pre_grad_ref, b_in_grad_ref,
    conv_ref, grad_in_ref, grad_out_ref,
):
    channels, hid = w_in_ref.shape
    conv_ref[...] = inner_ref[...]
    add_columns(conv_ref, kernel_ref, near_ref, far_ref, tile_h, tw, channels)
    conv = jnp.concatenate([conv_ref[t, :, :][:, :width] for t, _, width in lane_tiles(channels)], axis=1)
    shifted = conv - jnp.mean(conv, axis=1, keepdims=True)
    inv_std = lax.rsqrt(jnp.mean(shifted * shifted, axis=1, keepdims=True) + EPS)
    normed = shifted * inv_std
    normed_ref[...] = normed
    inv_std_ref[...] = jnp.broadcast_to(inv_std, inv_std_ref.shape)
    act = (normed * gain_ref[...] + ln_bias_ref[...]).astype(LINK)
    branch_grad = branch_grad_ref[...]
    width = 256
    for j in range(hid // width):
        cols = pl.ds(j * width, width)
        pre = dot(act, w_in_ref[:, cols], ((1,), (0,))) + b_in_ref[cols][None, :]
        square = pre * pre
        tanh = jnp.tanh(ROOT_2_PI * (pre + 0.044715 * (pre * square)))
        half = 0.5 * (1.0 + tanh)
        hidden = (pre * half).astype(LINK)
        slope = half + (0.5 * ROOT_2_PI) * pre * (1.0 - tanh * tanh) * (1.0 + (3 * 0.044715) * square)
        pre_grad = hidden_grad_ref[:, cols] * slope
        b_in_grad_ref[:, cols] = jnp.sum(pre_grad, axis=0, keepdims=True)
        pre_grad = pre_grad.astype(LINK)
        hidden_ref[:, cols] = hidden
        pre_grad_ref[:, cols] = pre_grad
        grad_in_ref[:, cols] = dot(act, pre_grad, ((0,), (0,)))
        grad_out_ref[:, cols] = dot(branch_grad, hidden, ((0,), (0,)))
    first = lax.axis_index("dp") == 0

    @pl.when(first)
    def _():
        keep_ref[...] = grad_in_ref[...]
        send_ref[...] = grad_out_ref[...].astype(LINK)

    @pl.when(jnp.logical_not(first))
    def _():
        keep_ref[...] = grad_out_ref[...]
        send_ref[...] = grad_in_ref[...].astype(LINK)


def norm_back_kernel(
    pre_grad_ref, w_in_ref, normed_ref, inv_std_ref, gain_ref, conv_grad_ref, sums_ref
):
    act_grad = dot(pre_grad_ref[...], w_in_ref[...], ((1,), (1,)))
    normed = normed_ref[...]
    scaled = act_grad * gain_ref[...]
    conv_grad = inv_std_ref[...][:, :1] * (
        scaled
        - jnp.mean(scaled, axis=1, keepdims=True)
        - normed * jnp.mean(scaled * normed, axis=1, keepdims=True)
    )
    conv_grad_ref[...] = conv_grad
    for i, value in enumerate((conv_grad, act_grad * normed, act_grad)):
        sums_ref[i : i + 1, :] = jnp.sum(value, axis=0, keepdims=True)


def lat_send_kernel(tw, keep_ref, other_ref, conv_grad_ref, send_ref, mine_ref):
    rows = mine_ref.shape[0]
    cells, channels = conv_grad_ref.shape
    lat = lax.axis_index("lat")
    mine = pl.ds(pl.multiple_of(lat * rows, 8), rows)
    theirs = pl.ds(pl.multiple_of((1 - lat) * rows, 8), rows)
    mine_ref[...] = keep_ref[mine, :] + other_ref[mine, :].astype(F32)
    send_ref[:rows, :] = (keep_ref[theirs, :] + other_ref[theirs, :].astype(F32)).astype(LINK)
    for r in range(3):
        tail = conv_grad_ref[pl.ds(cells - (3 - r) * tw, tw), :]
        head = conv_grad_ref[pl.ds(r * tw, tw), :]
        send_ref[pl.ds(rows, tw), pl.ds(r * SLOT, channels)] = jnp.where(
            lat == 0, tail, head
        ).astype(LINK)


def kernel_grad_kernel(
    tile_h, tw, start_ref, lat_ref, near_ref, far_ref, conv_grad_ref, sums_ref, b_in_grad_ref,
    hidden_ref, w_out_ref, b_out_ref, full_ref, cot_ref, scale_ref,
    send_ref, block_out_hbm, out_ref, padded_ref, shifts_ref, block_out_ref, sems,
):
    channels = conv_grad_ref.shape[1]
    branch = dot(hidden_ref[...], w_out_ref[...], ((1,), (1,))) + b_out_ref[...]
    full = full_ref[...]
    out_grad = cot_ref[...].astype(F32) * full
    scale = scale_ref[...]
    block_out_ref[...] = (full * (start_ref[...].astype(F32) + scale * branch)).astype(LINK)
    write = copies(((block_out_ref, block_out_hbm),), sems)
    places = tap_slots(49 + 5)
    out_ref[...] = jnp.zeros(out_ref.shape, F32)
    sums = [sums_ref[i : i + 1, :] for i in range(3)] + [
        jnp.sum(value, axis=0, keepdims=True) for value in (out_grad * scale, out_grad * branch)
    ]
    for i, value in enumerate(sums):
        row, lane = places[49 + i]
        out_ref[row : row + 1, pl.ds(lane, channels)] = value
    top, bottom = lat_rows(lambda r: lat_ref[pl.ds(r * tw, tw), :], tw)
    fill_center(
        padded_ref, lambda h: start_ref[pl.ds(h * tw, tw), :].astype(F32), tile_h, tw, top, bottom
    )
    read_edges(padded_ref, tw, channels, near_ref, far_ref, 0)
    shift_all(padded_ref, shifts_ref, tile_h, tw)
    for q in range(7):

        def step(h, totals):
            base = pl.multiple_of(h * tw, 8)
            grad = conv_grad_ref[pl.ds(base, tw), :]
            rows = shifts_ref[q, pl.ds(base, 7 * tw), :]
            new = []
            for r in range(7):
                product = grad * rows[r * tw : (r + 1) * tw]
                new.append(totals[r] + sum(product[8 * p : 8 * p + 8] for p in range(tw // 8)))
            return tuple(new)

        totals = lax.fori_loop(
            0, tile_h, step, tuple(jnp.zeros((8, channels), F32) for _ in range(7))
        )
        for r in range(7):
            row, lane = places[r * 7 + q]
            out_ref[row : row + 1, pl.ds(lane, channels)] = jnp.sum(
                totals[r], axis=0, keepdims=True
            )
    out_ref[out_ref.shape[0] - 1 :, :] = b_in_grad_ref[...]
    send_ref[...] = out_ref[...].astype(LINK)
    write[0].wait()


def lon_send_kernel(
    tile_h, tw, mine_ref, lat_ref, conv_grad_ref, small_ref, small_other_ref,
    near_ref, across_ref, far_ref, own_ref, total_ref, smalls_ref, padded_ref,
):
    rows = mine_ref.shape[0]
    chunk = rows // 4
    total_ref[...] = mine_ref[...] + lat_ref[:rows, :].astype(F32)
    smalls_ref[...] = small_ref[...].astype(F32) + small_other_ref[...].astype(F32)
    lon = lax.axis_index("lon")

    def fill(ref, index):
        ref[:chunk, :] = total_ref[pl.ds(pl.multiple_of(index * chunk, 8), chunk), :].astype(
            ref.dtype
        )
        ref[chunk : chunk + 8, :] = smalls_ref[pl.ds(pl.multiple_of(index * 8, 8), 8), :].astype(
            ref.dtype
        )

    fill(near_ref, lon ^ 1)
    fill(across_ref, lon ^ 2)
    fill(far_ref, lon ^ 3)
    fill(own_ref, lon)
    channels = conv_grad_ref.shape[1]
    top, bottom = lat_rows(lambda r: lat_ref[pl.ds(rows, tw), pl.ds(r * SLOT, channels)], tw)
    fill_center(
        padded_ref, lambda h: conv_grad_ref[pl.ds(h * tw, tw), :], tile_h, tw, top, bottom
    )
    write_edges(padded_ref, tw, channels, near_ref, far_ref, chunk + 8)


def reduce_kernel(factor, own_ref, near_ref, across_ref, far_ref, out_ref):
    rows = own_ref.shape[0]
    total = own_ref[...] + near_ref[:rows, :].astype(F32)
    total = total + across_ref[...].astype(F32) + far_ref[:rows, :].astype(F32)
    out_ref[...] = (total * factor).astype(LINK)


def field_grad_kernel(
    tile_h, tw, row, rows, conv_grad_ref, lat_ref, near_ref, far_ref, kernel_ref, full_ref, cot_ref,
    out_hbm, padded_ref, shifts_ref, conv_ref, result_ref, sems,
):
    channels = conv_grad_ref.shape[1]
    top, bottom = lat_rows(lambda r: lat_ref[pl.ds(rows, tw), pl.ds(r * SLOT, channels)], tw)
    fill_center(
        padded_ref, lambda h: conv_grad_ref[pl.ds(h * tw, tw), :], tile_h, tw, top, bottom
    )
    read_edges(padded_ref, tw, channels, near_ref, far_ref, row)
    shift_all(padded_ref, shifts_ref, tile_h, tw)
    convolve(shifts_ref, kernel_ref, conv_ref, tile_h, tw, True)
    full = full_ref[...]
    result_ref[...] = (full * (cot_ref[...].astype(F32) * full + conv_ref[...])).astype(LINK)
    copies(((result_ref, out_hbm),), sems)[0].wait()


def lon_gather_kernel(own_ref, near_ref, across_ref, far_ref, send_ref, mine_ref):
    chunk = own_ref.shape[0] - 8
    rows = 4 * chunk
    lon = lax.axis_index("lon")
    for step, ref in enumerate((own_ref, near_ref, across_ref, far_ref)):
        index = lon ^ step
        send_ref[pl.ds(pl.multiple_of(index * chunk, 8), chunk), :] = ref[:chunk, :]
        send_ref[pl.ds(pl.multiple_of(rows + index * 8, 8), 8), :] = ref[chunk:, :]
    mine_ref[...] = send_ref[:rows, :]


def unpack_kernel(
    own_ref, lat_ref, dp_own_ref, dp_lat_ref,
    grad_in_ref, grad_out_ref, kernel_ref, bias_ref, gain_ref, ln_bias_ref, b_in_ref, b_out_ref, scale_ref,
    small_ref,
):
    rows = dp_own_ref.shape[0]
    channels = kernel_ref.shape[2]
    lat = lax.axis_index("lat")
    first = lax.axis_index("dp") == 0
    here = pl.ds(pl.multiple_of(lat * rows, 8), rows)
    there = pl.ds(pl.multiple_of((1 - lat) * rows, 8), rows)

    def put(mine_ref, other_ref):
        mine_ref[here, :] = own_ref[:rows, :].astype(F32)
        mine_ref[there, :] = lat_ref[:rows, :].astype(F32)
        other_ref[here, :] = dp_own_ref[...].astype(F32)
        other_ref[there, :] = dp_lat_ref[:rows, :].astype(F32)

    @pl.when(first)
    def _():
        put(grad_in_ref, grad_out_ref)

    @pl.when(jnp.logical_not(first))
    def _():
        put(grad_out_ref, grad_in_ref)

    small_ref[...] = own_ref[rows:, :].astype(F32) + lat_ref[rows:, :].astype(F32)
    places = tap_slots(54)
    for i in range(49):
        row, lane = places[i]
        kernel_ref[i // 7, i % 7 : i % 7 + 1, :] = small_ref[row : row + 1, pl.ds(lane, channels)]
    for i, ref in enumerate((bias_ref, gain_ref, ln_bias_ref, b_out_ref, scale_ref)):
        row, lane = places[49 + i]
        ref[...] = small_ref[row : row + 1, pl.ds(lane, channels)]
    b_in_ref[...] = small_ref[small_ref.shape[0] - 1, :]


def swap(axis, step):
    return [(i, i ^ step) for i in range(lax.axis_size(axis))]


def fast_body(
    fields, cotangent, ocean_mask, dw_kernel, dw_bias, ln_gain, ln_bias, w_in, b_in, w_out, b_out,
    layer_scale,
):
    snapshots, tile_h, tw, channels = fields.shape
    cells = tile_h * tw
    hid = w_in.shape[1]
    fields2 = fields.reshape(cells, channels)
    cot2 = cotangent.reshape(cells, channels)
    row = lambda vector: vector.reshape(1, -1)
    w_out_t = w_out.T
    padded = pltpu.VMEM((-(-channels // 128), PAD_ROWS * STRIDE, 128), F32)
    shifts_shape = (7, (tile_h + 6) * tw, channels)
    tile = (cells, channels)

    sems = lambda count: pltpu.SemaphoreType.DMA((count,))
    start, edge, full = call(
        functools.partial(prepare_kernel, tw),
        [(tile, LINK), ((3 * tw, channels), LINK), (tile, F32)],
        (fields2, ocean_mask),
        scratch=[pltpu.VMEM(tile, LINK), pltpu.VMEM(ocean_mask.shape, jnp.int32), sems(2)],
        hbm=(0, 1),
    )
    lat_in = lax.ppermute(edge, "lat", swap("lat", 1))
    held = (
        cot2, row(layer_scale), w_out_t, dw_kernel, row(dw_bias), row(ln_gain), row(ln_bias), w_in, b_in,
        row(b_out),
    )
    loaded = call(
        load_kernel,
        [(array.shape, array.dtype) for array in held] + [(tile, LINK), ((cells, hid), F32)],
        (full, *held),
        2 * cells * channels * hid,
        scratch=[sems(len(held))],
        hbm=range(1, 1 + len(held)),
    )
    cot2, scale, w_out_v, taps, bias, gain, ln_b, w_in_v, b_in_v, b_out_v = loaded[: len(held)]
    branch_grad, hidden_grad = loaded[len(held) :]
    near, far = call(
        functools.partial(edges_kernel, tile_h, tw),
        [((PAD_ROWS, 3 * SLOT), LINK)] * 2,
        (start, lat_in, bias),
        scratch=[padded],
    )
    near_in = lax.ppermute(near, "lon", swap("lon", 1))
    far_in = lax.ppermute(far, "lon", swap("lon", 3))
    split = (-(-channels // 128), cells, 128)
    (inner,) = call(
        functools.partial(inner_conv_kernel, tile_h, tw),
        [(split, F32)],
        (start, lat_in, taps, bias),
        100 * cells * channels,
        scratch=[padded, pltpu.VMEM(shifts_shape, F32), pltpu.VMEM(tile, F32)],
    )
    send, keep, normed, inv_std, hidden, pre_grad, b_in_grad = call(
        functools.partial(main_kernel, tile_h, tw),
        [
            ((channels, hid), LINK),
            ((channels, hid), F32),
            (tile, F32),
            ((cells, 128), F32),
            ((cells, hid), LINK),
            ((cells, hid), LINK),
            ((1, hid), F32),
        ],
        (inner, near_in, far_in, taps, gain, ln_b, branch_grad, hidden_grad, w_in_v, b_in_v),
        6 * cells * channels * hid,
        scratch=[
            pltpu.VMEM(split, F32),
            pltpu.VMEM((channels, hid), F32),
            pltpu.VMEM((channels, hid), F32),
        ],
    )
    other = lax.ppermute(send, "dp", swap("dp", 1))
    conv_grad, sums = call(
        norm_back_kernel,
        [(tile, F32), ((3, channels), F32)],
        (pre_grad, w_in_v, normed, inv_std, gain),
        2 * cells * channels * hid,
    )
    half = channels // 2
    lat_send, mine = call(
        functools.partial(lat_send_kernel, tw),
        [((half + tw, hid), LINK), ((half, hid), F32)],
        (keep, other, conv_grad),
    )
    lat_got = lax.ppermute(lat_send, "lat", swap("lat", 1))
    small_rows = 32
    small, block_out = call(
        functools.partial(kernel_grad_kernel, tile_h, tw),
        [((small_rows, hid), LINK), (tile, LINK)],
        (
            start, lat_in, near_in, far_in, conv_grad, sums, b_in_grad, hidden, w_out_v, b_out_v, full,
            cot2, scale,
        ),
        100 * cells * channels + 2 * cells * channels * hid,
        scratch=[
            pltpu.VMEM((small_rows, hid), F32),
            padded,
            pltpu.VMEM(shifts_shape, F32),
            pltpu.VMEM(tile, LINK),
            sems(1),
        ],
        hbm_out=(1,),
    )
    small_other = lax.ppermute(small, "dp", swap("dp", 1))
    chunk = half // 4
    part = chunk + 8
    near, across, far, own = call(
        functools.partial(lon_send_kernel, tile_h, tw),
        [
            ((part + PAD_ROWS, hid), LINK),
            ((part, hid), LINK),
            ((part + PAD_ROWS, hid), LINK),
            ((part, hid), F32),
        ],
        (mine, lat_got, conv_grad, small, small_other),
        scratch=[pltpu.VMEM((half, hid), F32), pltpu.VMEM((small_rows, hid), F32), padded],
    )
    near_got = lax.ppermute(near, "lon", swap("lon", 1))
    across_got = lax.ppermute(across, "lon", swap("lon", 2))
    far_got = lax.ppermute(far, "lon", swap("lon", 3))
    members = lax.axis_size("lon") * lax.axis_size("lat") * lax.axis_size("dp")
    factor = 1.0 / math.sqrt(snapshots * cells * members)
    (reduced,) = call(
        functools.partial(reduce_kernel, factor),
        [((part, hid), LINK)],
        (own, near_got, across_got, far_got),
    )
    gathered = [lax.ppermute(reduced, "lon", swap("lon", step)) for step in (1, 2, 3)]
    (field_grad,) = call(
        functools.partial(field_grad_kernel, tile_h, tw, part, half),
        [(tile, LINK)],
        (conv_grad, lat_got, near_got, far_got, taps, full, cot2),
        100 * cells * channels,
        scratch=[
            padded, pltpu.VMEM(shifts_shape, F32), pltpu.VMEM(tile, F32), pltpu.VMEM(tile, LINK), sems(1),
        ],
        hbm_out=(0,),
    )
    send, mine = call(
        lon_gather_kernel,
        [((half + small_rows, hid), LINK), ((half, hid), LINK)],
        (reduced, *gathered),
    )
    lat_got = lax.ppermute(send, "lat", swap("lat", 1))
    dp_own = lax.ppermute(mine, "dp", swap("dp", 1))
    lat_got, field_grad = lax.optimization_barrier((lat_got, field_grad))
    dp_lat = lax.ppermute(lat_got, "dp", swap("dp", 1))
    vector = ((1, channels), F32)
    outs = call(
        unpack_kernel,
        [
            ((channels, hid), F32),
            ((channels, hid), F32),
            (dw_kernel.shape, F32),
            vector, vector, vector,
            ((hid,), F32),
            vector, vector,
        ],
        (send, lat_got, dp_own, dp_lat),
        scratch=[pltpu.VMEM((small_rows, hid), F32)],
    )
    grad_in, grad_out, grad_kernel, bias_g, gain_g, ln_b_g, b_in_g, b_out_g, scale_g = outs
    return (
        block_out.reshape(fields.shape),
        field_grad.reshape(fields.shape),
        grad_kernel,
        bias_g.reshape(-1),
        gain_g.reshape(-1),
        ln_b_g.reshape(-1),
        grad_in,
        b_in_g,
        grad_out.T,
        b_out_g.reshape(-1),
        scale_g.reshape(-1),
    )


def solution(mesh):
    sizes = dict(mesh.shape)
    paired = sizes["lat"] == 2 and sizes["lon"] == 4 and sizes["dp"] == 2
    return jax.shard_map(
        fast_body if paired else body,
        mesh=mesh,
        in_specs=(
            P(("groups", "dp"), "lat", "lon", None),
            P(("groups", "dp"), "lat", "lon", None),
            P("lat", "lon"),
            P(),
            P(),
            P(),
            P(),
            P(),
            P(),
            P(),
            P(),
            P(),
        ),
        out_specs=(
            P(("groups", "dp"), "lat", "lon", None),
            P(("groups", "dp"), "lat", "lon", None),
            P("groups", None, None),
            P("groups"),
            P("groups"),
            P("groups"),
            P("groups", None),
            P("groups"),
            P("groups", None),
            P("groups"),
            P("groups"),
        ),
        check_vma=False,
    )
```

```python
import functools
import math

import jax
import jax.numpy as jnp
from jax import lax
from jax.experimental import pallas as pl
from jax.experimental.pallas import tpu as pltpu
from jax.sharding import PartitionSpec as P

EPS = 1e-06


def padded_2(block, sides, width, periodic):
    for axis, dim in sides:
        count = lax.axis_size(axis)
        if count == 2 and not periodic:
            block = padded_pair(block, axis, dim, width)
            continue
        forward = [(i, i + 1) for i in range(count - 1)]
        if periodic:
            forward.append((count - 1, 0))
        backward = [(target, source) for source, target in forward]
        low = lax.ppermute(
            lax.slice_in_dim(block, block.shape[dim] - width, None, axis=dim), axis, forward
        )
        high = lax.ppermute(lax.slice_in_dim(block, 0, width, axis=dim), axis, backward)
        block = jnp.concatenate([low, block, high], axis=dim)
    return block


def padded_pair(block, axis, dim, width):
    first = lax.axis_index(axis) == 0
    head = lax.slice_in_dim(block, 0, width, axis=dim)
    tail = lax.slice_in_dim(block, block.shape[dim] - width, None, axis=dim)
    other = lax.ppermute(jnp.where(first, tail, head), axis, [(0, 1), (1, 0)])
    none = jnp.zeros_like(other)
    return jnp.concatenate(
        [jnp.where(first, none, other), block, jnp.where(first, other, none)], axis=dim
    )


LANES = 256
LINK = jnp.bfloat16


def to_rows(piece):
    rows, columns = piece.shape
    blocks = -(-columns // LANES)
    piece = jnp.pad(piece, ((0, 0), (0, blocks * LANES - columns)))
    return [piece[:, b * LANES : (b + 1) * LANES] for b in range(blocks)]


def from_rows(rows_array, start, rows, columns):
    blocks = -(-columns // LANES)
    parts = [rows_array[start + b * rows : start + (b + 1) * rows] for b in range(blocks)]
    return jnp.concatenate(parts, axis=1)[:, :columns], start + blocks * rows


def rounds_of(count):
    if count & (count - 1) == 0 and count <= 4:
        return [([(i, i ^ step) for i in range(count)], lambda me, s=step: (me ^ s, me ^ s)) for step in range(1, count)]
    return [
        (
            [(i, (i + step) % count) for i in range(count)],
            lambda me, s=step: (lax.rem(me + s, count), lax.rem(me + count - s, count)),
        )
        for step in range(1, count)
    ]


def scatter_sum(rows_array, axis):
    count = lax.axis_size(axis)
    size = rows_array.shape[0] // count
    me = lax.axis_index(axis)
    total = lax.dynamic_slice_in_dim(rows_array, me * size, size, axis=0)
    arrived = []
    for perm, ends in rounds_of(count):
        target, _ = ends(me)
        piece = lax.dynamic_slice_in_dim(rows_array, target * size, size, axis=0)
        arrived.append(lax.ppermute(piece.astype(LINK), axis, perm))
    for piece in arrived:
        total = total + piece.astype(jnp.float32)
    return total


def gather_rows(piece, axis):
    count = lax.axis_size(axis)
    size = piece.shape[0]
    me = lax.axis_index(axis)
    whole = jnp.zeros((count * size,) + piece.shape[1:], piece.dtype)
    whole = lax.dynamic_update_slice_in_dim(whole, piece, me * size, axis=0)
    for perm, ends in rounds_of(count):
        _, source = ends(me)
        other = lax.ppermute(piece, axis, perm)
        whole = lax.dynamic_update_slice_in_dim(whole, other, source * size, axis=0)
    return whole


def sum_over(pieces, axes, factor):
    members = math.prod(lax.axis_size(axis) for axis in axes)
    stacked = sum((to_rows(piece) for piece in pieces), [])
    rows = sum(part.shape[0] for part in stacked)
    quantum = members * 8
    extra = -rows % quantum
    stacked.append(jnp.zeros((extra, LANES), jnp.float32))
    total = jnp.concatenate(stacked, axis=0)
    for axis in axes:
        total = scatter_sum(total, axis)
    total = (total * factor).astype(LINK)
    for axis in reversed(axes):
        total = gather_rows(total, axis)
    total = total.astype(jnp.float32)
    out, start = [], 0
    for piece in pieces:
        value, start = from_rows(total, start, *piece.shape)
        out.append(value)
    return out


def depthwise(padded, kernel, tile_h, tile_w):
    total = jnp.zeros(padded.shape[:-3] + (tile_h, tile_w, padded.shape[-1]), jnp.float32)
    for row_off in range(7):
        for col_off in range(7):
            total = (
                total
                + padded[..., row_off : row_off + tile_h, col_off : col_off + tile_w, :]
                * kernel[row_off, col_off]
            )
    return total


def depthwise_back(padded, kernel, tile_h, tile_w):
    total = jnp.zeros(padded.shape[:-3] + (tile_h, tile_w, padded.shape[-1]), jnp.float32)
    for row_off in range(7):
        for col_off in range(7):
            total = (
                total
                + padded[
                    ..., 6 - row_off : 6 - row_off + tile_h, 6 - col_off : 6 - col_off + tile_w, :
                ]
                * kernel[row_off, col_off]
            )
    return total


def kernel_grad(grad, padded, tile_h, tile_w):
    lead = tuple(range(grad.ndim - 1))
    return jnp.stack(
        [
            jnp.stack(
                [
                    jnp.sum(
                        grad
                        * padded[..., row_off : row_off + tile_h, col_off : col_off + tile_w, :],
                        axis=lead,
                    )
                    for col_off in range(7)
                ]
            )
            for row_off in range(7)
        ]
    )


def gelu_tanh(values):
    return jax.nn.gelu(values, approximate=True)


def mlp_pass(act_rows, out_grad, w_in, b_in, w_out, b_out, layer_scale):
    pre = jnp.dot(act_rows, w_in, preferred_element_type=jnp.float32) + b_in
    hidden, gelu_back = jax.vjp(gelu_tanh, pre)
    hidden_b = hidden.astype(jnp.bfloat16)
    branch = jnp.dot(hidden_b, w_out, preferred_element_type=jnp.float32) + b_out
    branch_grad = out_grad * layer_scale
    branch_b = branch_grad.astype(jnp.bfloat16)
    hidden_grad = jnp.dot(branch_b, w_out.T, preferred_element_type=jnp.float32)
    pre_grad = gelu_back(hidden_grad)[0]
    pre_b = pre_grad.astype(jnp.bfloat16)
    act_grad = jnp.dot(pre_b, w_in.T, preferred_element_type=jnp.float32)
    grads = (
        jnp.dot(act_rows.T, pre_b, preferred_element_type=jnp.float32),
        jnp.sum(pre_grad, axis=0),
        jnp.dot(branch_b.T, hidden_b, preferred_element_type=jnp.float32),
        jnp.sum(branch_grad, axis=0),
        jnp.sum(out_grad * branch, axis=0),
    )
    return (branch, act_grad, grads)


def body(
    fields,
    cotangent,
    ocean_mask,
    dw_kernel,
    dw_bias,
    ln_gain,
    ln_bias,
    w_in,
    b_in,
    w_out,
    b_out,
    layer_scale,
):
    snapshots, tile_h, tile_w, channels = fields.shape
    cells = tile_h * tile_w
    ocean = ocean_mask.astype(jnp.float32)[None, :, :, None]
    start_b = fields * ocean_mask.astype(jnp.bfloat16)[None, :, :, None]
    lat_ext = padded_2(start_b, (("lat", 1),), 3, False)
    padded = padded_2(lat_ext, (("lon", 2),), 3, True).astype(jnp.float32)
    start = start_b.astype(jnp.float32)
    conv_out = depthwise(padded, dw_kernel, tile_h, tile_w) + dw_bias
    center = jnp.mean(conv_out, axis=-1, keepdims=True)
    shifted = conv_out - center
    inv_std = lax.rsqrt(jnp.mean(shifted * shifted, axis=-1, keepdims=True) + EPS)
    normed = shifted * inv_std
    act = (normed * ln_gain + ln_bias).astype(jnp.bfloat16)
    out_grad = cotangent.astype(jnp.float32) * ocean
    flat_branch, flat_act_grad, mlp_sums = mlp_pass(
        act.reshape(-1, channels),
        out_grad.reshape(-1, channels),
        w_in,
        b_in,
        w_out,
        b_out,
        layer_scale,
    )
    branch = flat_branch.reshape(fields.shape)
    act_grad = flat_act_grad.reshape(fields.shape)
    block_out = (ocean * (start + layer_scale * branch)).astype(jnp.bfloat16)
    scaled = act_grad * ln_gain
    conv_grad = inv_std * (
        scaled
        - jnp.mean(scaled, axis=-1, keepdims=True)
        - normed * jnp.mean(scaled * normed, axis=-1, keepdims=True)
    )
    grad_lat = padded_2(conv_grad.astype(jnp.bfloat16), (("lat", 1),), 3, False).astype(
        conv_grad.dtype
    )
    grad_padded = padded_2(grad_lat.astype(jnp.bfloat16), (("lon", 2),), 3, True).astype(
        grad_lat.dtype
    )
    field_grad = (
        ocean * (out_grad + depthwise_back(grad_padded, dw_kernel, tile_h, tile_w))
    ).astype(jnp.bfloat16)
    lead = (0, 1, 2)
    local = (
        kernel_grad(conv_grad, padded, tile_h, tile_w),
        jnp.sum(conv_grad, axis=lead),
        jnp.sum(act_grad * normed, axis=lead),
        jnp.sum(act_grad, axis=lead),
    ) + mlp_sums
    members = lax.axis_size("lon") * lax.axis_size("lat") * lax.axis_size("dp")
    factor = 1.0 / math.sqrt(snapshots * cells * members)
    hid = w_in.shape[1]
    smalls = jnp.concatenate(
        [
            local[0].reshape(-1, channels),
            jnp.stack([local[1], local[2], local[3], local[7], local[8]]),
            local[5].reshape(-1, channels),
        ],
        axis=0,
    )
    got = sum_over([local[4], local[6], smalls], ("dp", "lat", "lon"), factor)
    taps = dw_kernel.shape[0] * dw_kernel.shape[1]
    small = got[2]
    finals = (
        small[:taps].reshape(dw_kernel.shape),
        small[taps],
        small[taps + 1],
        small[taps + 2],
        got[0],
        small[taps + 5 :].reshape(hid),
        got[1].T,
        small[taps + 3],
        small[taps + 4],
    )
    return (
        block_out,
        field_grad,
        finals[0],
        finals[1],
        finals[2],
        finals[3],
        finals[4],
        finals[5],
        finals[6],
        finals[7],
        finals[8],
    )


VMEM = pl.BlockSpec(memory_space=pltpu.VMEM)
HBM = pl.BlockSpec(memory_space=pltpu.HBM)
PARAMS = pltpu.CompilerParams(vmem_limit_bytes=20 << 20)
F32 = jnp.float32
SLOT = 256
STRIDE = 32
CENTER = 8
PAD_ROWS = 24
ROOT_2_PI = math.sqrt(2 / math.pi)


def call(kernel, outs, args, flops=0, scratch=(), hbm=(), hbm_out=()):
    moved = sum(a.size * a.dtype.itemsize for a in args) + sum(
        math.prod(s) * jnp.dtype(d).itemsize for s, d in outs
    )
    args = [
        pltpu.with_memory_space_constraint(a, pltpu.HBM) if i in hbm else a for i, a in enumerate(args)
    ]
    return pl.pallas_call(
        kernel,
        out_shape=tuple(jax.ShapeDtypeStruct(s, d) for s, d in outs),
        in_specs=[HBM if i in hbm else VMEM for i in range(len(args))],
        out_specs=tuple(HBM if i in hbm_out else VMEM for i in range(len(outs))),
        scratch_shapes=list(scratch),
        compiler_params=PARAMS,
        cost_estimate=pl.CostEstimate(flops=flops, bytes_accessed=moved, transcendentals=0),
    )(*args)


def copies(pairs, sems):
    started = [
        pltpu.make_async_copy(source, target, sems.at[i]) for i, (source, target) in enumerate(pairs)
    ]
    for copy in started:
        copy.start()
    return started


def dot(a, b, dims):
    return lax.dot_general(a, b, (dims, ((), ())), preferred_element_type=F32)


def tap_slots(taps):
    return [((i // 24) * 8 + i % 8, ((i % 24) // 8) * SLOT) for i in range(taps)]


def mask_full(mask_ref, cells, channels):
    tile_w = mask_ref.shape[1]
    index = lax.broadcasted_iota(jnp.int32, (cells, mask_ref.shape[0]), 0)
    of_row = lax.div(index, tile_w) == lax.broadcasted_iota(jnp.int32, index.shape, 1)
    mask = mask_ref[...].astype(F32).astype(LINK)
    rows = dot(of_row.astype(F32).astype(LINK), mask, ((1,), (0,)))
    index = lax.broadcasted_iota(jnp.int32, rows.shape, 0)
    of_col = lax.rem(index, tile_w) == lax.broadcasted_iota(jnp.int32, rows.shape, 1)
    picked = jnp.where(of_col, rows, 0.0).astype(LINK)
    return dot(picked, jnp.ones((tile_w, channels), LINK), ((1,), (0,)))


def prepare_kernel(tw, fields_hbm, mask_hbm, start_ref, edge_ref, full_ref, fields_ref, mask_ref, sems):
    fetch = copies(((mask_hbm, mask_ref), (fields_hbm, fields_ref)), sems)
    cells, channels = fields_ref.shape
    fetch[0].wait()
    full = mask_full(mask_ref, cells, channels)
    full_ref[...] = full
    fetch[1].wait()
    start_ref[...] = (fields_ref[...].astype(F32) * full).astype(LINK)
    first = lax.axis_index("lat") == 0
    edge_ref[...] = jnp.where(first, start_ref[cells - 3 * tw :], start_ref[: 3 * tw])


def load_kernel(full_ref, *refs):
    count = (len(refs) - 3) // 2
    sources, targets = refs[:count], refs[count : 2 * count]
    branch_grad_ref, hidden_grad_ref, sems = refs[2 * count :]
    fetch = copies(tuple(zip(sources, targets)), sems)
    cot_ref, scale_ref, w_out_ref = targets[:3]
    for copy in fetch[:3]:
        copy.wait()
    grad = (cot_ref[...].astype(F32) * full_ref[...] * scale_ref[...]).astype(LINK)
    branch_grad_ref[...] = grad
    hidden_grad_ref[...] = dot(grad, w_out_ref[...], ((1,), (0,)))
    for copy in fetch[3:]:
        copy.wait()


def lane_tiles(channels):
    return [(t, t * 128, min(128, channels - t * 128)) for t in range(-(-channels // 128))]


def put_rows(padded_ref, row, values):
    for t, lane, width in lane_tiles(values.shape[1]):
        padded_ref[t, pl.ds(row, values.shape[0]), pl.ds(0, width)] = values[:, lane : lane + width]


def fill_center(padded_ref, value_of_row, tile_h, tw, top, bottom):
    for h in range(tile_h):
        put_rows(padded_ref, (h + 3) * STRIDE + CENTER, value_of_row(h))
    for r in range(3):
        put_rows(padded_ref, r * STRIDE + CENTER, top(r))
        put_rows(padded_ref, (tile_h + 3 + r) * STRIDE + CENTER, bottom(r))


def write_edges(padded_ref, tw, channels, near_ref, far_ref, row):
    even = lax.rem(lax.axis_index("lon"), 2) == 0
    for c in range(3):
        for t, lane, width in lane_tiles(channels):
            left = padded_ref[t, pl.ds(CENTER + c, PAD_ROWS, stride=STRIDE), :]
            right = padded_ref[t, pl.ds(CENTER + tw - 3 + c, PAD_ROWS, stride=STRIDE), :]
            place = pl.ds(row, PAD_ROWS), pl.ds(c * SLOT + lane, width)
            near_ref[place] = jnp.where(even, right, left)[:, :width].astype(LINK)
            far_ref[place] = jnp.where(even, left, right)[:, :width].astype(LINK)


def read_edges(padded_ref, tw, channels, near_ref, far_ref, row):
    even = lax.rem(lax.axis_index("lon"), 2) == 0
    for c in range(3):
        for t, lane, width in lane_tiles(channels):
            place = pl.ds(row, PAD_ROWS), pl.ds(c * SLOT + lane, 128)
            near = near_ref[place].astype(F32)
            far = far_ref[place].astype(F32)
            left = pl.ds(CENTER - 3 + c, PAD_ROWS, stride=STRIDE)
            right = pl.ds(CENTER + tw + c, PAD_ROWS, stride=STRIDE)
            padded_ref[t, left, :] = jnp.where(even, far, near)
            padded_ref[t, right, :] = jnp.where(even, near, far)


def lat_rows(read, tw):
    first = lax.axis_index("lat") == 0

    def top(r):
        rows = read(r).astype(F32)
        return jnp.where(first, jnp.zeros_like(rows), rows)

    def bottom(r):
        rows = read(r).astype(F32)
        return jnp.where(first, rows, jnp.zeros_like(rows))

    return top, bottom


def shift_all(padded_ref, shifts_ref, tile_h, tw):
    for q in range(7):
        for h in range(tile_h + 6):
            for t, lane, width in lane_tiles(shifts_ref.shape[2]):
                shifts_ref[q, pl.ds(h * tw, tw), pl.ds(lane, width)] = padded_ref[
                    t, pl.ds(h * STRIDE + CENTER - 3 + q, tw), pl.ds(0, width)
                ]


def convolve(shifts_ref, kernel_ref, out_ref, tile_h, tw, flip):
    block = 2

    def step(i, carry):
        base = pl.multiple_of(i * block * tw, 8)
        total = jnp.zeros((block * tw, out_ref.shape[1]), F32)
        for q in range(7):
            rows = shifts_ref[q, pl.ds(base, (block + 6) * tw), :]
            for r in range(7):
                tap = kernel_ref[6 - r, 6 - q : 7 - q, :] if flip else kernel_ref[r, q : q + 1, :]
                total = total + rows[r * tw : (r + block) * tw] * tap
        out_ref[pl.ds(base, block * tw), :] = total
        return carry

    lax.fori_loop(0, tile_h // block, step, 0)


def edges_kernel(tile_h, tw, start_ref, lat_ref, loaded_ref, near_ref, far_ref, padded_ref):
    top, bottom = lat_rows(lambda r: lat_ref[pl.ds(r * tw, tw), :], tw)
    fill_center(
        padded_ref, lambda h: start_ref[pl.ds(h * tw, tw), :].astype(F32), tile_h, tw, top, bottom
    )
    write_edges(padded_ref, tw, start_ref.shape[1], near_ref, far_ref, 0)


def inner_conv_kernel(
    tile_h, tw, start_ref, lat_ref, kernel_ref, bias_ref, out_ref, padded_ref, shifts_ref, conv_ref
):
    top, bottom = lat_rows(lambda r: lat_ref[pl.ds(r * tw, tw), :], tw)
    fill_center(
        padded_ref, lambda h: start_ref[pl.ds(h * tw, tw), :].astype(F32), tile_h, tw, top, bottom
    )
    blank = jnp.zeros((PAD_ROWS, 128), F32)
    for t in range(padded_ref.shape[0]):
        for c in range(3):
            padded_ref[t, pl.ds(CENTER - 3 + c, PAD_ROWS, stride=STRIDE), :] = blank
            padded_ref[t, pl.ds(CENTER + tw + c, PAD_ROWS, stride=STRIDE), :] = blank
    shift_all(padded_ref, shifts_ref, tile_h, tw)
    convolve(shifts_ref, kernel_ref, conv_ref, tile_h, tw, False)
    conv = conv_ref[...] + bias_ref[...]
    for t, lane, width in lane_tiles(conv.shape[1]):
        out_ref[t, :, pl.ds(0, width)] = conv[:, lane : lane + width]


def add_columns(conv_ref, kernel_ref, near_ref, far_ref, tile_h, tw, channels):
    even = lax.rem(lax.axis_index("lon"), 2) == 0
    for t, lane, width in lane_tiles(channels):
        left, right = [], []
        for c in range(3):
            place = pl.ds(0, PAD_ROWS), pl.ds(c * SLOT + lane, width)
            near = near_ref[place].astype(F32)
            far = far_ref[place].astype(F32)
            left.append(jnp.where(even, far, near))
            right.append(jnp.where(even, near, far))
        for w in range(3):
            for col, halo, taps in (
                (w, left, [(q, w + q) for q in range(3 - w)]),
                (tw - 1 - w, right, [(6 - q, 2 - w - q) for q in range(3 - w)]),
            ):
                rows = pl.ds(col, tile_h, stride=tw)
                total = conv_ref[t, rows, :][:, :width]
                for q, c in taps:
                    for r in range(7):
                        tap = kernel_ref[r, q : q + 1, pl.ds(lane, width)]
                        total = total + halo[c][r : r + tile_h] * tap
                conv_ref[t, rows, pl.ds(0, width)] = total


def main_kernel(
    tile_h, tw,
    inner_ref, near_ref, far_ref, kernel_ref, gain_ref, ln_bias_ref, branch_grad_ref, hidden_grad_ref,
    w_in_ref, b_in_ref,
    send_ref, keep_ref, normed_ref, inv_std_ref, hidden_ref, pre_grad_ref, b_in_grad_ref,
    conv_ref, grad_in_ref, grad_out_ref,
):
    channels, hid = w_in_ref.shape
    conv_ref[...] = inner_ref[...]
    add_columns(conv_ref, kernel_ref, near_ref, far_ref, tile_h, tw, channels)
    conv = jnp.concatenate([conv_ref[t, :, :][:, :width] for t, _, width in lane_tiles(channels)], axis=1)
    shifted = conv - jnp.mean(conv, axis=1, keepdims=True)
    inv_std = lax.rsqrt(jnp.mean(shifted * shifted, axis=1, keepdims=True) + EPS)
    normed = shifted * inv_std
    normed_ref[...] = normed
    inv_std_ref[...] = jnp.broadcast_to(inv_std, inv_std_ref.shape)
    act = (normed * gain_ref[...] + ln_bias_ref[...]).astype(LINK)
    branch_grad = branch_grad_ref[...]
    width = 256
    for j in range(hid // width):
        cols = pl.ds(j * width, width)
        pre = dot(act, w_in_ref[:, cols], ((1,), (0,))) + b_in_ref[cols][None, :]
        square = pre * pre
        tanh = jnp.tanh(ROOT_2_PI * (pre + 0.044715 * (pre * square)))
        half = 0.5 * (1.0 + tanh)
        hidden = (pre * half).astype(LINK)
        slope = half + (0.5 * ROOT_2_PI) * pre * (1.0 - tanh * tanh) * (1.0 + (3 * 0.044715) * square)
        pre_grad = hidden_grad_ref[:, cols] * slope
        b_in_grad_ref[:, cols] = jnp.sum(pre_grad, axis=0, keepdims=True)
        pre_grad = pre_grad.astype(LINK)
        hidden_ref[:, cols] = hidden
        pre_grad_ref[:, cols] = pre_grad
        grad_in_ref[:, cols] = dot(act, pre_grad, ((0,), (0,)))
        grad_out_ref[:, cols] = dot(branch_grad, hidden, ((0,), (0,)))
    first = lax.axis_index("dp") == 0

    @pl.when(first)
    def _():
        keep_ref[...] = grad_in_ref[...]
        send_ref[...] = grad_out_ref[...].astype(LINK)

    @pl.when(jnp.logical_not(first))
    def _():
        keep_ref[...] = grad_out_ref[...]
        send_ref[...] = grad_in_ref[...].astype(LINK)


def norm_back_kernel(
    pre_grad_ref, w_in_ref, normed_ref, inv_std_ref, gain_ref, conv_grad_ref, sums_ref
):
    act_grad = dot(pre_grad_ref[...], w_in_ref[...], ((1,), (1,)))
    normed = normed_ref[...]
    scaled = act_grad * gain_ref[...]
    conv_grad = inv_std_ref[...][:, :1] * (
        scaled
        - jnp.mean(scaled, axis=1, keepdims=True)
        - normed * jnp.mean(scaled * normed, axis=1, keepdims=True)
    )
    conv_grad_ref[...] = conv_grad
    for i, value in enumerate((conv_grad, act_grad * normed, act_grad)):
        sums_ref[i : i + 1, :] = jnp.sum(value, axis=0, keepdims=True)


def lat_send_kernel(tw, keep_ref, other_ref, conv_grad_ref, send_ref, mine_ref):
    rows = mine_ref.shape[0]
    cells, channels = conv_grad_ref.shape
    lat = lax.axis_index("lat")
    mine = pl.ds(pl.multiple_of(lat * rows, 8), rows)
    theirs = pl.ds(pl.multiple_of((1 - lat) * rows, 8), rows)
    mine_ref[...] = keep_ref[mine, :] + other_ref[mine, :].astype(F32)
    send_ref[:rows, :] = (keep_ref[theirs, :] + other_ref[theirs, :].astype(F32)).astype(LINK)
    for r in range(3):
        tail = conv_grad_ref[pl.ds(cells - (3 - r) * tw, tw), :]
        head = conv_grad_ref[pl.ds(r * tw, tw), :]
        send_ref[pl.ds(rows, tw), pl.ds(r * SLOT, channels)] = jnp.where(
            lat == 0, tail, head
        ).astype(LINK)


def kernel_grad_kernel(
    tile_h, tw, start_ref, lat_ref, near_ref, far_ref, conv_grad_ref, sums_ref, b_in_grad_ref,
    hidden_ref, w_out_ref, b_out_ref, full_ref, cot_ref, scale_ref,
    send_ref, block_out_hbm, out_ref, padded_ref, shifts_ref, block_out_ref, sems,
):
    channels = conv_grad_ref.shape[1]
    branch = dot(hidden_ref[...], w_out_ref[...], ((1,), (1,))) + b_out_ref[...]
    full = full_ref[...]
    out_grad = cot_ref[...].astype(F32) * full
    scale = scale_ref[...]
    block_out_ref[...] = (full * (start_ref[...].astype(F32) + scale * branch)).astype(LINK)
    write = copies(((block_out_ref, block_out_hbm),), sems)
    places = tap_slots(49 + 5)
    out_ref[...] = jnp.zeros(out_ref.shape, F32)
    sums = [sums_ref[i : i + 1, :] for i in range(3)] + [
        jnp.sum(value, axis=0, keepdims=True) for value in (out_grad * scale, out_grad * branch)
    ]
    for i, value in enumerate(sums):
        row, lane = places[49 + i]
        out_ref[row : row + 1, pl.ds(lane, channels)] = value
    top, bottom = lat_rows(lambda r: lat_ref[pl.ds(r * tw, tw), :], tw)
    fill_center(
        padded_ref, lambda h: start_ref[pl.ds(h * tw, tw), :].astype(F32), tile_h, tw, top, bottom
    )
    read_edges(padded_ref, tw, channels, near_ref, far_ref, 0)
    shift_all(padded_ref, shifts_ref, tile_h, tw)
    for q in range(7):

        def step(h, totals):
            base = pl.multiple_of(h * tw, 8)
            grad = conv_grad_ref[pl.ds(base, tw), :]
            rows = shifts_ref[q, pl.ds(base, 7 * tw), :]
            new = []
            for r in range(7):
                product = grad * rows[r * tw : (r + 1) * tw]
                new.append(totals[r] + sum(product[8 * p : 8 * p + 8] for p in range(tw // 8)))
            return tuple(new)

        totals = lax.fori_loop(
            0, tile_h, step, tuple(jnp.zeros((8, channels), F32) for _ in range(7))
        )
        for r in range(7):
            row, lane = places[r * 7 + q]
            out_ref[row : row + 1, pl.ds(lane, channels)] = jnp.sum(
                totals[r], axis=0, keepdims=True
            )
    out_ref[out_ref.shape[0] - 1 :, :] = b_in_grad_ref[...]
    send_ref[...] = out_ref[...].astype(LINK)
    write[0].wait()


def lon_send_kernel(
    tile_h, tw, mine_ref, lat_ref, conv_grad_ref, small_ref, small_other_ref,
    near_ref, across_ref, far_ref, own_ref, total_ref, smalls_ref, padded_ref,
):
    rows = mine_ref.shape[0]
    chunk = rows // 4
    total_ref[...] = mine_ref[...] + lat_ref[:rows, :].astype(F32)
    smalls_ref[...] = small_ref[...].astype(F32) + small_other_ref[...].astype(F32)
    lon = lax.axis_index("lon")

    def fill(ref, index):
        ref[:chunk, :] = total_ref[pl.ds(pl.multiple_of(index * chunk, 8), chunk), :].astype(
            ref.dtype
        )
        ref[chunk : chunk + 8, :] = smalls_ref[pl.ds(pl.multiple_of(index * 8, 8), 8), :].astype(
            ref.dtype
        )

    fill(near_ref, lon ^ 1)
    fill(across_ref, lon ^ 2)
    fill(far_ref, lon ^ 3)
    fill(own_ref, lon)
    channels = conv_grad_ref.shape[1]
    top, bottom = lat_rows(lambda r: lat_ref[pl.ds(rows, tw), pl.ds(r * SLOT, channels)], tw)
    fill_center(
        padded_ref, lambda h: conv_grad_ref[pl.ds(h * tw, tw), :], tile_h, tw, top, bottom
    )
    write_edges(padded_ref, tw, channels, near_ref, far_ref, chunk + 8)


def reduce_kernel(factor, own_ref, near_ref, across_ref, far_ref, out_ref):
    rows = own_ref.shape[0]
    total = own_ref[...] + near_ref[:rows, :].astype(F32)
    total = total + across_ref[...].astype(F32) + far_ref[:rows, :].astype(F32)
    out_ref[...] = (total * factor).astype(LINK)


def field_grad_kernel(
    tile_h, tw, row, rows, conv_grad_ref, lat_ref, near_ref, far_ref, kernel_ref, full_ref, cot_ref,
    out_hbm, padded_ref, shifts_ref, conv_ref, result_ref, sems,
):
    channels = conv_grad_ref.shape[1]
    top, bottom = lat_rows(lambda r: lat_ref[pl.ds(rows, tw), pl.ds(r * SLOT, channels)], tw)
    fill_center(
        padded_ref, lambda h: conv_grad_ref[pl.ds(h * tw, tw), :], tile_h, tw, top, bottom
    )
    read_edges(padded_ref, tw, channels, near_ref, far_ref, row)
    shift_all(padded_ref, shifts_ref, tile_h, tw)
    convolve(shifts_ref, kernel_ref, conv_ref, tile_h, tw, True)
    full = full_ref[...]
    result_ref[...] = (full * (cot_ref[...].astype(F32) * full + conv_ref[...])).astype(LINK)
    copies(((result_ref, out_hbm),), sems)[0].wait()


def lon_gather_kernel(own_ref, near_ref, across_ref, far_ref, send_ref, mine_ref):
    chunk = own_ref.shape[0] - 8
    rows = 4 * chunk
    lon = lax.axis_index("lon")
    for step, ref in enumerate((own_ref, near_ref, across_ref, far_ref)):
        index = lon ^ step
        send_ref[pl.ds(pl.multiple_of(index * chunk, 8), chunk), :] = ref[:chunk, :]
        send_ref[pl.ds(pl.multiple_of(rows + index * 8, 8), 8), :] = ref[chunk:, :]
    mine_ref[...] = send_ref[:rows, :]


def unpack_kernel(
    own_ref, lat_ref, dp_own_ref, dp_lat_ref,
    grad_in_ref, grad_out_ref, kernel_ref, bias_ref, gain_ref, ln_bias_ref, b_in_ref, b_out_ref, scale_ref,
    small_ref,
):
    rows = dp_own_ref.shape[0]
    channels = kernel_ref.shape[2]
    lat = lax.axis_index("lat")
    first = lax.axis_index("dp") == 0
    here = pl.ds(pl.multiple_of(lat * rows, 8), rows)
    there = pl.ds(pl.multiple_of((1 - lat) * rows, 8), rows)

    def put(mine_ref, other_ref):
        mine_ref[here, :] = own_ref[:rows, :].astype(F32)
        mine_ref[there, :] = lat_ref[:rows, :].astype(F32)
        other_ref[here, :] = dp_own_ref[...].astype(F32)
        other_ref[there, :] = dp_lat_ref[:rows, :].astype(F32)

    @pl.when(first)
    def _():
        put(grad_in_ref, grad_out_ref)

    @pl.when(jnp.logical_not(first))
    def _():
        put(grad_out_ref, grad_in_ref)

    small_ref[...] = own_ref[rows:, :].astype(F32) + lat_ref[rows:, :].astype(F32)
    places = tap_slots(54)
    for i in range(49):
        row, lane = places[i]
        kernel_ref[i // 7, i % 7 : i % 7 + 1, :] = small_ref[row : row + 1, pl.ds(lane, channels)]
    for i, ref in enumerate((bias_ref, gain_ref, ln_bias_ref, b_out_ref, scale_ref)):
        row, lane = places[49 + i]
        ref[...] = small_ref[row : row + 1, pl.ds(lane, channels)]
    b_in_ref[...] = small_ref[small_ref.shape[0] - 1, :]


def swap(axis, step):
    return [(i, i ^ step) for i in range(lax.axis_size(axis))]


def fast_body(
    fields, cotangent, ocean_mask, dw_kernel, dw_bias, ln_gain, ln_bias, w_in, b_in, w_out, b_out,
    layer_scale,
):
    snapshots, tile_h, tw, channels = fields.shape
    cells = tile_h * tw
    hid = w_in.shape[1]
    fields2 = fields.reshape(cells, channels)
    cot2 = cotangent.reshape(cells, channels)
    row = lambda vector: vector.reshape(1, -1)
    w_out_t = w_out.T
    padded = pltpu.VMEM((-(-channels // 128), PAD_ROWS * STRIDE, 128), F32)
    shifts_shape = (7, (tile_h + 6) * tw, channels)
    tile = (cells, channels)

    sems = lambda count: pltpu.SemaphoreType.DMA((count,))
    start, edge, full = call(
        functools.partial(prepare_kernel, tw),
        [(tile, LINK), ((3 * tw, channels), LINK), (tile, F32)],
        (fields2, ocean_mask),
        scratch=[pltpu.VMEM(tile, LINK), pltpu.VMEM(ocean_mask.shape, jnp.int32), sems(2)],
        hbm=(0, 1),
    )
    lat_in = lax.ppermute(edge, "lat", swap("lat", 1))
    held = (
        cot2, row(layer_scale), w_out_t, dw_kernel, row(dw_bias), row(ln_gain), row(ln_bias), w_in, b_in,
        row(b_out),
    )
    loaded = call(
        load_kernel,
        [(array.shape, array.dtype) for array in held] + [(tile, LINK), ((cells, hid), F32)],
        (full, *held),
        2 * cells * channels * hid,
        scratch=[sems(len(held))],
        hbm=range(1, 1 + len(held)),
    )
    cot2, scale, w_out_v, taps, bias, gain, ln_b, w_in_v, b_in_v, b_out_v = loaded[: len(held)]
    branch_grad, hidden_grad = loaded[len(held) :]
    near, far = call(
        functools.partial(edges_kernel, tile_h, tw),
        [((PAD_ROWS, 3 * SLOT), LINK)] * 2,
        (start, lat_in, bias),
        scratch=[padded],
    )
    near_in = lax.ppermute(near, "lon", swap("lon", 1))
    far_in = lax.ppermute(far, "lon", swap("lon", 3))
    split = (-(-channels // 128), cells, 128)
    (inner,) = call(
        functools.partial(inner_conv_kernel, tile_h, tw),
        [(split, F32)],
        (start, lat_in, taps, bias),
        100 * cells * channels,
        scratch=[padded, pltpu.VMEM(shifts_shape, F32), pltpu.VMEM(tile, F32)],
    )
    send, keep, normed, inv_std, hidden, pre_grad, b_in_grad = call(
        functools.partial(main_kernel, tile_h, tw),
        [
            ((channels, hid), LINK),
            ((channels, hid), F32),
            (tile, F32),
            ((cells, 128), F32),
            ((cells, hid), LINK),
            ((cells, hid), LINK),
            ((1, hid), F32),
        ],
        (inner, near_in, far_in, taps, gain, ln_b, branch_grad, hidden_grad, w_in_v, b_in_v),
        6 * cells * channels * hid,
        scratch=[
            pltpu.VMEM(split, F32),
            pltpu.VMEM((channels, hid), F32),
            pltpu.VMEM((channels, hid), F32),
        ],
    )
    other = lax.ppermute(send, "dp", swap("dp", 1))
    conv_grad, sums = call(
        norm_back_kernel,
        [(tile, F32), ((3, channels), F32)],
        (pre_grad, w_in_v, normed, inv_std, gain),
        2 * cells * channels * hid,
    )
    half = channels // 2
    lat_send, mine = call(
        functools.partial(lat_send_kernel, tw),
        [((half + tw, hid), LINK), ((half, hid), F32)],
        (keep, other, conv_grad),
    )
    lat_got = lax.ppermute(lat_send, "lat", swap("lat", 1))
    small_rows = 32
    small, block_out = call(
        functools.partial(kernel_grad_kernel, tile_h, tw),
        [((small_rows, hid), LINK), (tile, LINK)],
        (
            start, lat_in, near_in, far_in, conv_grad, sums, b_in_grad, hidden, w_out_v, b_out_v, full,
            cot2, scale,
        ),
        100 * cells * channels + 2 * cells * channels * hid,
        scratch=[
            pltpu.VMEM((small_rows, hid), F32),
            padded,
            pltpu.VMEM(shifts_shape, F32),
            pltpu.VMEM(tile, LINK),
            sems(1),
        ],
        hbm_out=(1,),
    )
    small_other = lax.ppermute(small, "dp", swap("dp", 1))
    chunk = half // 4
    part = chunk + 8
    near, across, far, own = call(
        functools.partial(lon_send_kernel, tile_h, tw),
        [
            ((part + PAD_ROWS, hid), LINK),
            ((part, hid), LINK),
            ((part + PAD_ROWS, hid), LINK),
            ((part, hid), F32),
        ],
        (mine, lat_got, conv_grad, small, small_other),
        scratch=[pltpu.VMEM((half, hid), F32), pltpu.VMEM((small_rows, hid), F32), padded],
    )
    near_got = lax.ppermute(near, "lon", swap("lon", 1))
    across_got = lax.ppermute(across, "lon", swap("lon", 2))
    far_got = lax.ppermute(far, "lon", swap("lon", 3))
    members = lax.axis_size("lon") * lax.axis_size("lat") * lax.axis_size("dp")
    factor = 1.0 / math.sqrt(snapshots * cells * members)
    (reduced,) = call(
        functools.partial(reduce_kernel, factor),
        [((part, hid), LINK)],
        (own, near_got, across_got, far_got),
    )
    gathered = [lax.ppermute(reduced, "lon", swap("lon", step)) for step in (1, 2, 3)]
    (field_grad,) = call(
        functools.partial(field_grad_kernel, tile_h, tw, part, half),
        [(tile, LINK)],
        (conv_grad, lat_got, near_got, far_got, taps, full, cot2),
        100 * cells * channels,
        scratch=[
            padded, pltpu.VMEM(shifts_shape, F32), pltpu.VMEM(tile, F32), pltpu.VMEM(tile, LINK), sems(1),
        ],
        hbm_out=(0,),
    )
    send, mine = call(
        lon_gather_kernel,
        [((half + small_rows, hid), LINK), ((half, hid), LINK)],
        (reduced, *gathered),
    )
    lat_got = lax.ppermute(send, "lat", swap("lat", 1))
    dp_own = lax.ppermute(mine, "dp", swap("dp", 1))
    lat_got, field_grad = lax.optimization_barrier((lat_got, field_grad))
    dp_lat = lax.ppermute(lat_got, "dp", swap("dp", 1))
    vector = ((1, channels), F32)
    outs = call(
        unpack_kernel,
        [
            ((channels, hid), F32),
            ((channels, hid), F32),
            (dw_kernel.shape, F32),
            vector, vector, vector,
            ((hid,), F32),
            vector, vector,
        ],
        (send, lat_got, dp_own, dp_lat),
        scratch=[pltpu.VMEM((small_rows, hid), F32)],
    )
    grad_in, grad_out, grad_kernel, bias_g, gain_g, ln_b_g, b_in_g, b_out_g, scale_g = outs
    return (
        block_out.reshape(fields.shape),
        field_grad.reshape(fields.shape),
        grad_kernel,
        bias_g.reshape(-1),
        gain_g.reshape(-1),
        ln_b_g.reshape(-1),
        grad_in,
        b_in_g,
        grad_out.T,
        b_out_g.reshape(-1),
        scale_g.reshape(-1),
    )


def solution(mesh):
    sizes = dict(mesh.shape)
    paired = sizes["lat"] == 2 and sizes["lon"] == 4 and sizes["dp"] == 2
    return jax.shard_map(
        fast_body if paired else body,
        mesh=mesh,
        in_specs=(
            P(("groups", "dp"), "lat", "lon", None),
            P(("groups", "dp"), "lat", "lon", None),
            P("lat", "lon"),
            P(),
            P(),
            P(),
            P(),
            P(),
            P(),
            P(),
            P(),
            P(),
        ),
        out_specs=(
            P(("groups", "dp"), "lat", "lon", None),
            P(("groups", "dp"), "lat", "lon", None),
            P("groups", None, None),
            P("groups"),
            P("groups"),
            P("groups"),
            P("groups", None),
            P("groups"),
            P("groups", None),
            P("groups"),
            P("groups"),
        ),
        check_vma=False,
    )
```
